32 devices in a mesh: grp: 2 (over y), gx: 16 (over z, x, core).
Axes of the slice: x: 2, y: 2, z: 4, core: 2. Of those that a mesh axis runs over, the one named last changes fastest.
Arguments:
- voltages: bfloat16 [2, 512, 2, 1, 2, 16384], P('grp', 'gx'), may hold values from -6 to 6
- tile_of: int32 [2, 32768], P(None, 'gx'), may hold values from -1 to 1, as said below
- cell_of: int32 [2, 32768], P(None, 'gx'), may hold values from 0 to 511
Outputs:
- image: float32 [2, 2, 4096, 4096], P('grp', None, 'gx')
The draws below stay inside these ranges and needn't reach their ends.
Inputs may be any that keep to these rules, and one draw needn't show every extreme that they name: `tile_of`: among the 2048 blocks of one coarse channel and one gx index, no tile is named more than 256 times, and one tile exactly 256 times; -1 marks blocks that no tile takes.
All inputs are finite; a program needn't handle non-finite values.
Results may differ from the reference program's by a relative error of at most 0.006.
Values may be sent and summed in bfloat16 or wider, within the bound.
No kernel may reach another device: no remote copies, remote signals or barrier semaphores. Data moves between devices by JAX's collectives and lax.ppermute only.
A program may use at most 128 MiB of HBM per device.

```python
import jax
import jax.numpy as jnp
from jax import lax

NFINE = 16384
AVG = 256
ST = 512
POL = 2
NSPEC = 1
NIN = 1024
BR = 16
BC = 128
TILE = 4096
COARSE = 2
OUT_DEV = 4
NB = 2048
NBLK = 32768
CAP = 256
SLAB = 256
CELLS = 512
N_GRP = 2
N_GX = 16


def draw_tile_of(key, part):
    keys = jax.random.split(key, COARSE * N_GX)

    def one_row(row_key):
        first, second, third = jax.random.split(row_key, 3)
        tiles = jnp.arange(N_GRP, dtype=jnp.int32)
        busiest = jax.random.randint(first, (), 0, N_GRP, dtype=jnp.int32)
        lower = jax.random.randint(second, (N_GRP,), 1, CAP // 2 + 1, dtype=jnp.int32)
        counts = jnp.where(tiles == busiest, CAP, lower).astype(jnp.int32)
        ends = jnp.cumsum(counts).astype(jnp.int32)
        position = jnp.arange(NB, dtype=jnp.int32)
        tile_at = jnp.sum((position[:, None] >= ends[None, :]).astype(jnp.int32), axis=1)
        tile_at = jnp.where(tile_at >= N_GRP, -1, tile_at).astype(jnp.int32)
        order = jax.random.permutation(third, NB).astype(jnp.int32)
        return jnp.zeros((NB,), jnp.int32).at[order].set(tile_at)
    rows = jax.vmap(one_row)(keys)
    return rows.reshape(COARSE, N_GX * NB).astype(jnp.int32)


def touch_ends(result, own_key, smallest, largest):
    dims = result.shape
    index_at = [jax.random.randint(jax.random.fold_in(own_key, axis), (), 0, dims[axis]) for axis in range(len(dims))]
    result = result.at[tuple(index_at)].set(smallest)
    longest = dims.index(max(dims))
    index_at[longest] = (index_at[longest] + 1) % dims[longest]
    return result.at[tuple(index_at)].set(largest)


def steps_of(key, extent, pieces, low, top_value):
    def one(dim, blocks):
        draws = jax.random.uniform(jax.random.fold_in(jax.random.fold_in(key, 6), dim), (blocks,), jnp.float32, low / len(pieces), top_value / len(pieces))
        return jnp.repeat(jnp.exp(draws), extent[dim] // blocks).reshape((-1,) + (1,) * (len(extent) - dim - 1))

    factor_of = one(*pieces[0])
    for cut in pieces[1:]:
        factor_of = factor_of * one(*cut)
    return factor_of


def centred(stream_key, extent, scale, most, cuts=(), kind=jnp.bfloat16):
    values = jax.random.normal(stream_key, extent, jnp.float32) * scale
    if len(cuts) > 0:
        values = steps_of(stream_key, extent, cuts, -0.22, 0.18) * values
    return jnp.clip(values, min=-most, max=most).astype(kind)


def setup_inputs(seed: int = 0) -> dict:
    splits = jax.random.split(jax.random.key(seed), 4)
    return {
        "voltages": centred(splits[0], (COARSE, ST, POL, NSPEC, 2, NFINE), 1.0, 6.0, ((0, 2), (1, 16))),
        "tile_of": draw_tile_of(jax.random.fold_in(splits[3], 71), 0),
        "cell_of": touch_ends(jax.random.randint(splits[2], (COARSE, NBLK), 0, CELLS), jax.random.fold_in(splits[2], 1), 0, CELLS - 1).astype(jnp.int32),
    }


def spectra_of(volt):
    field = volt[:, :, :, 0].astype(jnp.float32) + 1j * volt[:, :, :, 1].astype(jnp.float32)
    spec = jnp.fft.fft(field, axis=-1, norm="ortho")
    return jnp.stack([jnp.real(spec), jnp.imag(spec)], axis=3).astype(jnp.bfloat16)


def blocks_of(spec):
    nout = NFINE // AVG
    grouped = spec.reshape(NIN, NSPEC, 2, nout, AVG).astype(jnp.float32)
    gram = jnp.einsum("psrof,qsxof->orpxq", grouped, grouped, precision=lax.Precision.HIGHEST)
    factor = 1.0 / (NSPEC * AVG) ** 0.5
    vis_re = (gram[:, 0, :, 0, :] + gram[:, 1, :, 1, :]) * factor
    vis_im = (gram[:, 1, :, 0, :] - gram[:, 0, :, 1, :]) * factor
    vis = jnp.stack([vis_re, vis_im], axis=1).astype(jnp.bfloat16)
    shaped = vis.reshape(N_GX, OUT_DEV, 2, NIN // BR, BR, NIN // BC, BC)
    return shaped.transpose(0, 1, 3, 5, 2, 4, 6).reshape(N_GX * NB, 2 * BR * BC)


def reference(voltages, tile_of, cell_of):
    total_cells = N_GRP * N_GX * CELLS

    def add_group(grid, inputs):
        volt, tiles, cells = inputs
        blocks = blocks_of(spectra_of(volt)).astype(jnp.float32)
        owner = jnp.arange(N_GX * NB, dtype=jnp.int32) // NB
        ids = ((tiles * N_GX + owner) * CELLS + cells).astype(jnp.int32)
        ids = jnp.where(tiles < 0, total_cells, ids).astype(jnp.int32)
        return grid.at[ids].add(blocks, mode="drop"), None

    start = jnp.zeros((total_cells, 2 * BR * BC), jnp.float32)
    grid, _ = lax.scan(add_group, start, (voltages, tile_of, cell_of))
    grid = grid.reshape(N_GRP, N_GX * CELLS, 2 * BR * BC)

    def image_of(cells_grid):
        field = cells_grid.reshape(N_GX, SLAB // BR, TILE // BC, 2, BR, BC)
        field = field.transpose(3, 0, 1, 4, 2, 5).reshape(2, TILE, TILE)
        rows = jnp.fft.ifft(field[0] + 1j * field[1], axis=1, norm="ortho")
        rows_re = lax.optimization_barrier(jnp.real(rows).astype(jnp.bfloat16)).astype(jnp.float32)
        rows_im = lax.optimization_barrier(jnp.imag(rows).astype(jnp.bfloat16)).astype(jnp.float32)
        cols = jnp.fft.ifft(rows_re + 1j * rows_im, axis=0, norm="ortho")
        return jnp.stack([jnp.real(cols).T, jnp.imag(cols).T]).astype(jnp.float32)

    return lax.map(image_of, grid)
```

```python
import functools
import math

import jax
import jax.numpy as jnp
import numpy as np
from jax import lax
from jax.experimental import pallas as pl
from jax.experimental.pallas import tpu as pltpu
from jax.sharding import PartitionSpec as P

FRADIX = 128
AVG = 256
BR = 16
BC = 128
TRADIX = 64
TILE = 4096
SUB = 8
PACK = 16
F32 = jnp.float32
BF16 = jnp.bfloat16


def halves(matrix):
    high = matrix.astype(np.float32).astype(BF16)
    low = (matrix - high.astype(np.float64)).astype(np.float32).astype(BF16)
    return high, low


def complex_table(angle, scale):
    cos, sin = scale * np.cos(angle), scale * np.sin(angle)
    return np.stack([np.stack([cos, -sin]), np.stack([sin, cos])])


def turn(product, period, sign):
    return sign * 2.0 * np.pi / period * (product % period)


def spectra_tables(n_gx, out_dev):
    index = np.arange(FRADIX)
    first = complex_table(turn(np.outer(index, index), FRADIX, -1.0), 1.0 / FRADIX)
    first = first.transpose(0, 2, 3, 1).reshape(2 * FRADIX, 2 * FRADIX)
    high, low = halves(first)
    first = np.concatenate([high, low], axis=1)
    angle = turn(np.outer(index, index), FRADIX * FRADIX, -1.0)
    twist = np.stack([np.cos(angle), np.sin(angle)]).astype(np.float32)
    second = complex_table(turn(np.outer(index, index), FRADIX, -1.0), 1.0)
    low_count = FRADIX // (n_gx * out_dev)
    second = second.reshape(2, 2, n_gx, out_dev, low_count, FRADIX)
    second = second.transpose(3, 2, 0, 4, 1, 5).reshape(2 * FRADIX, 2 * FRADIX)
    high, low = halves(second)
    second = np.concatenate([high, low, high], axis=1)
    return first, twist, second


def row_tables(n_gx):
    cols = TILE // BC
    k1, w = np.arange(cols), np.arange(BC)
    angle = turn(np.outer(k1, w), TILE, 1.0)
    twist = np.stack([np.cos(angle), np.sin(angle)]).astype(np.float32)
    second = complex_table(turn(np.outer(w, w), BC, 1.0), 1.0 / math.sqrt(TILE))
    second = second.transpose(2, 0, 1, 3).reshape(2 * BC, 2 * BC)
    high, low = halves(second)
    return twist, np.concatenate([high, low, high], axis=1)


def column_tables(n_gx):
    count = TILE // BR
    blocks = count // n_gx
    index = np.arange(count)
    first = complex_table(turn(np.outer(index, index), count, 1.0), 1.0 / math.sqrt(TILE))
    first = first.reshape(2, 2, n_gx, blocks, count)
    first = first.transpose(2, 1, 3, 0, 4).reshape(2 * count, 2 * count)
    high, low = halves(first)
    angle = turn(np.outer(np.arange(BR), index), TILE, 1.0)
    twist = np.stack([np.cos(angle), np.sin(angle)]).astype(np.float32)
    return np.concatenate([high, low], axis=0), twist


def times(value, factor):
    re, im = value
    c, s = factor
    return (re * c - im * s, re * s + im * c)


def fixed_turn(value, step, count, sign):
    re, im = value
    step = step % count
    if step == 0:
        return value
    if 4 * step == count:
        return (-im, re) if sign > 0 else (im, -re)
    angle = sign * 2.0 * math.pi * step / count
    c, s = math.cos(angle), math.sin(angle)
    if 8 * step == count:
        return ((re - im) * c, (re + im) * c) if sign > 0 else ((re + im) * c, (im - re) * c)
    if 8 * step == 3 * count:
        h = abs(c)
        return ((-re - im) * h, (re - im) * h) if sign > 0 else ((im - re) * h, (-re - im) * h)
    return (re * c - im * s, re * s + im * c)


def butterflies(values, sign):
    count = len(values)
    if count == 1:
        return values
    even = butterflies(values[0::2], sign)
    odd = butterflies(values[1::2], sign)
    out = [None] * count
    for k in range(count // 2):
        turned = fixed_turn(odd[k], k, count, sign)
        out[k] = (even[k][0] + turned[0], even[k][1] + turned[1])
        out[k + count // 2] = (even[k][0] - turned[0], even[k][1] - turned[1])
    return out


def split_value(value):
    high = value.astype(BF16)
    return high, (value - high.astype(F32)).astype(BF16)


def dot_nt(left, right):
    return lax.dot_general(left, right, (((1,), (1,)), ((), ())), preferred_element_type=F32)


def dot_tn(left, right):
    return lax.dot_general(left, right, (((0,), (0,)), ((), ())), preferred_element_type=F32)


def spectra_kernel(n_gx, out_dev, v_ref, first_ref, twist_ref, second_ref, *rest):
    out_refs, scratch = rest[:out_dev], rest[out_dev]
    rows = 2 * FRADIX

    def one(i, carry):
        v = v_ref[i]
        y = jnp.dot(first_ref[...], jnp.concatenate([v, v], axis=0), preferred_element_type=F32)
        re, im = times((y[:FRADIX], y[FRADIX:]), (twist_ref[0], twist_ref[1]))
        high, low = split_value(jnp.concatenate([re, im], axis=1))
        z = dot_nt(second_ref[...], jnp.concatenate([high, high, low], axis=1))
        scratch[pl.ds(pl.multiple_of(i * rows, rows), rows), :] = z
        return carry

    lax.fori_loop(0, PACK, one, 0, unroll=2)
    per = rows // (out_dev * n_gx)
    for o in range(out_dev):
        for d in range(n_gx):
            for t in range(per):
                row = (o * n_gx + d) * per + t
                piece = scratch[pl.ds(row, PACK, stride=rows), :]
                out_refs[o][d, :, t * FRADIX : (t + 1) * FRADIX] = piece.astype(BF16)


def spectra_call(volts, n_gx, out_dev):
    inputs = volts.shape[0]
    first, twist, second = spectra_tables(n_gx, out_dev)
    depth = 2 * AVG
    whole = lambda x: pl.BlockSpec(x.shape, lambda i: (0,) * x.ndim)
    return pl.pallas_call(
        functools.partial(spectra_kernel, n_gx, out_dev),
        grid=(inputs // PACK,),
        in_specs=[
            pl.BlockSpec((PACK, 2 * FRADIX, FRADIX), lambda i: (i, 0, 0)),
            whole(first),
            whole(twist),
            whole(second),
        ],
        out_specs=[pl.BlockSpec((n_gx, PACK, depth), lambda i: (0, i, 0))] * out_dev,
        out_shape=[jax.ShapeDtypeStruct((n_gx, inputs, depth), BF16)] * out_dev,
        scratch_shapes=[pltpu.VMEM((PACK * 2 * FRADIX, FRADIX), F32)],
        name="spectra",
    )(volts, first, twist, second)


def gram_kernel(first_call, cells, factor, count_ref, list_ref, *rest):
    if first_call:
        mine_ref, other_ref, out_ref, vis, grid, sem = rest
    else:
        mine_ref, other_ref, in_ref, out_ref, vis, grid, sem = rest
    nin, depth = mine_ref.shape
    half = depth // 2
    if first_call:
        def clear(i, carry):
            grid[:, pl.ds(i * SUB, SUB)] = jnp.zeros((2, SUB, BR, BC), F32)
            return carry

        lax.fori_loop(0, cells // SUB, clear, 0)
    else:
        load = pltpu.make_async_copy(in_ref, grid, sem)
        load.start()
    panel = 2 * BC
    for which, x_ref in enumerate((mine_ref, other_ref)):
        def one(p, carry):
            base = pl.multiple_of(p * panel, panel)
            x = x_ref[pl.ds(base, panel), :]
            swapped = jnp.concatenate([x[:, half:], -x[:, :half]], axis=1)
            left = jnp.concatenate([x, swapped], axis=0)
            gram = (dot_nt(left, x_ref[...]) * factor).astype(BF16)
            for e in range(nin // BC):
                vis[0, e, pl.ds(base, panel), :] = gram[:panel, e * BC : (e + 1) * BC]
                vis[1, e, pl.ds(base, panel), :] = gram[panel:, e * BC : (e + 1) * BC]
            return carry

        lax.fori_loop(0, nin // panel, one, 0)
        if which == 0 and not first_call:
            load.wait()

        def place(s, carry):
            code = list_ref[which, s]
            cell = lax.rem(code, cells)
            block = lax.div(code, cells)
            e = lax.rem(block, nin // BC)
            row = pl.multiple_of(lax.div(block, nin // BC) * BR, BR)
            for part in range(2):
                grid[part, cell] += vis[part, e, pl.ds(row, BR), :].astype(F32)
            return carry

        lax.fori_loop(0, count_ref[which], place, 0)
    store = pltpu.make_async_copy(grid, out_ref, sem)
    store.start()
    store.wait()


def gram_call(counts, lists, mine, other, grid, cells, factor):
    first_call = grid is None
    shape = (2, cells, BR, BC)
    nin, depth = mine.shape
    any_spec = pl.BlockSpec(memory_space=pl.ANY)
    vmem = pl.BlockSpec(memory_space=pltpu.VMEM)
    smem = pl.BlockSpec(memory_space=pltpu.SMEM)
    args = (counts, lists, mine, other) + (() if first_call else (grid,))
    flops = 2 * 2 * 2 * nin * nin * depth
    return pl.pallas_call(
        functools.partial(gram_kernel, first_call, cells, factor),
        in_specs=[smem, smem, vmem, vmem] + ([] if first_call else [any_spec]),
        out_specs=any_spec,
        out_shape=jax.ShapeDtypeStruct(shape, F32),
        scratch_shapes=[
            pltpu.VMEM((2, nin // BC, nin, BC), BF16),
            pltpu.VMEM(shape, F32),
            pltpu.SemaphoreType.DMA,
        ],
        input_output_aliases={} if first_call else {4: 0},
        cost_estimate=pl.CostEstimate(flops=flops, transcendentals=0, bytes_accessed=2**24),
        name="gram",
    )(*args)


def row_first_kernel(grid_ref, twist_ref, high_ref, low_ref, scratch):
    cols = TILE // BC
    for h in range(BR // SUB):
        rows = slice(h * SUB, (h + 1) * SUB)
        values = [(grid_ref[0, 0, c, rows], grid_ref[1, 0, c, rows]) for c in range(cols)]
        values = butterflies(values, 1.0)
        for k in range(cols):
            factor = (twist_ref[0, k : k + 1, :], twist_ref[1, k : k + 1, :])
            re, im = times(values[k], factor)
            at = slice(k * BR + h * SUB, k * BR + (h + 1) * SUB)
            scratch[at, :BC] = re
            scratch[at, BC:] = im
    high, low = split_value(scratch[...])
    high_ref[0] = high
    low_ref[0] = low


def row_first_call(grid, twist):
    _, blocks, cols, _, _ = grid.shape
    shape = jax.ShapeDtypeStruct((blocks, cols * BR, 2 * BC), BF16)
    out = pl.BlockSpec((1, cols * BR, 2 * BC), lambda i: (i, 0, 0))
    return pl.pallas_call(
        row_first_kernel,
        grid=(blocks,),
        in_specs=[
            pl.BlockSpec((2, 1, cols, BR, BC), lambda i: (0, i, 0, 0, 0)),
            pl.BlockSpec(twist.shape, lambda i: (0, 0, 0)),
        ],
        out_specs=[out, out],
        out_shape=[shape, shape],
        scratch_shapes=[pltpu.VMEM((cols * BR, 2 * BC), F32)],
        name="row_first",
    )(grid, twist)


def row_second_kernel(high_ref, low_ref, second_ref, out_ref, scratch):
    blocks, lanes, _ = high_ref.shape
    rows = 2 * BC

    def one(b, carry):
        for u in range(2):
            high, low = high_ref[2 * b + u], low_ref[2 * b + u]
            z = dot_nt(second_ref[...], jnp.concatenate([high, high, low], axis=1))
            scratch[pl.ds(pl.multiple_of((2 * b + u) * rows, rows), rows), :] = z
        return carry

    lax.fori_loop(0, blocks // 2, one, 0)
    n_gx, lows, _, _ = out_ref.shape
    for d in range(n_gx):
        for k in range(lows):
            for part in range(2):
                row = (d * lows + k) * 2 + part
                piece = scratch[pl.ds(row, blocks, stride=rows), :]
                out_ref[d, k, part * blocks : (part + 1) * blocks, :] = piece.astype(BF16)


def row_second_call(high, low, second, n_gx, chunk):
    blocks = high.shape[0]
    lanes = SUB * BR
    lows = BC // n_gx
    take = pl.BlockSpec((blocks, lanes, 2 * BC), lambda i: (0, chunk, 0))
    return pl.pallas_call(
        row_second_kernel,
        grid=(1,),
        in_specs=[take, take, pl.BlockSpec(second.shape, lambda i: (0, 0))],
        out_specs=pl.BlockSpec((n_gx, lows, 2 * blocks, lanes), lambda i: (0, 0, 0, 0)),
        out_shape=jax.ShapeDtypeStruct((n_gx, lows, 2 * blocks, lanes), BF16),
        scratch_shapes=[pltpu.VMEM((blocks * 2 * BC, lanes), F32)],
        cost_estimate=pl.CostEstimate(flops=2**31, transcendentals=0, bytes_accessed=2**22),
        name="row_second",
    )(high, low, second)


def column_kernel(alias, data_ref, first_ref, twist_ref, *rest):
    out_ref, scratch = rest[-2], rest[-1]
    n_gx, _, rows, lanes = data_ref.shape
    data = data_ref[:, 0].reshape(n_gx * rows, lanes)
    mixed = dot_tn(jnp.concatenate([data, data], axis=0), first_ref[...])
    count = TILE // BR
    for b in range(2 * count // BC):
        scratch[b * lanes : (b + 1) * lanes, :] = mixed[:, b * BC : (b + 1) * BC]
    for b in range(count // BC):
        values = []
        for r in range(BR):
            value = (
                scratch[pl.ds(b * lanes + r, SUB, stride=BR), :],
                scratch[pl.ds((count // BC + b) * lanes + r, SUB, stride=BR), :],
            )
            lane = slice(b * BC, (b + 1) * BC)
            values.append(times(value, (twist_ref[0, r : r + 1, lane], twist_ref[1, r : r + 1, lane])))
        values = butterflies(values, 1.0)
        for k in range(BR):
            lane = slice(k * count + b * BC, k * count + (b + 1) * BC)
            out_ref[0, 0, 0, :, lane] = values[k][0]
            out_ref[1, 0, 0, :, lane] = values[k][1]


def column_call(data, first, twist, image, chunk, chunks):
    n_gx, lows, rows, lanes = data.shape
    alias = image is not None
    shape = (2, lows, chunks, SUB, TILE)
    return pl.pallas_call(
        functools.partial(column_kernel, alias),
        grid=(lows,),
        in_specs=[
            pl.BlockSpec((n_gx, 1, rows, lanes), lambda i: (0, i, 0, 0)),
            pl.BlockSpec(first.shape, lambda i: (0, 0)),
            pl.BlockSpec(twist.shape, lambda i: (0, 0, 0)),
        ]
        + ([pl.BlockSpec(memory_space=pl.ANY)] if alias else []),
        out_specs=pl.BlockSpec((2, 1, 1, SUB, TILE), lambda i: (0, i, chunk, 0, 0)),
        out_shape=jax.ShapeDtypeStruct(shape, F32),
        scratch_shapes=[pltpu.VMEM((2 * (TILE // BR) // BC * lanes, BC), F32)],
        input_output_aliases={3: 0} if alias else {},
        cost_estimate=pl.CostEstimate(flops=2**30, transcendentals=0, bytes_accessed=2**22),
        name="column",
    )(data, first, twist, *((image,) if alias else ()))


def work_lists(tile_of, cell_of, me, out_dev, cells):
    groups, blocks = tile_of.shape
    per = blocks // out_dev
    taken = (tile_of == me).reshape(groups, out_dev, per)
    number = taken.astype(jnp.int32)
    rank = jnp.cumsum(number, axis=2) - number
    slot = jnp.where(taken, rank, -1)
    code = jnp.arange(per, dtype=jnp.int32) * cells + cell_of.reshape(groups, out_dev, per)
    hit = jnp.arange(per, dtype=jnp.int32)[:, None] == slot[:, :, None, :]
    lists = jnp.sum(jnp.where(hit, code[:, :, None, :], 0), axis=3)
    return jnp.sum(number, axis=2), lists


def pair_plan(voltages, tile_of, cell_of):
    n_gx = lax.axis_size("gx")
    _, st_dev, pols, spectra, parts, fine = voltages.shape
    inputs = st_dev * pols
    out_dev = fine // (n_gx * AVG)
    cells = (TILE // n_gx // BR) * (TILE // BC)
    blocks = TILE // n_gx // BR
    cols = TILE // BC
    me = lax.axis_index("grp")
    counts, lists = work_lists(tile_of, cell_of, me, out_dev, cells)
    swap = jnp.where(me == 0, jnp.arange(2), jnp.arange(2)[::-1])
    counts, lists = jnp.take(counts, swap, axis=0), jnp.take(lists, swap, axis=0)

    volts = voltages.reshape(inputs, 2, FRADIX, FRADIX).transpose(0, 2, 1, 3)
    volts = volts.reshape(inputs, 2 * FRADIX, FRADIX)
    spec = spectra_call(volts, n_gx, out_dev)
    grid = None
    for o in range(out_dev):
        mine = lax.all_to_all(spec[o], "gx", split_axis=0, concat_axis=0, tiled=True)
        mine = mine.reshape(n_gx * inputs, 2 * AVG)
        other = lax.ppermute(mine, "grp", [(0, 1), (1, 0)])
        factor = 1.0 / math.sqrt(spectra * AVG)
        grid = gram_call(counts[:, o], lists[:, o], mine, other, grid, cells, factor)
    twist, second = row_tables(n_gx)
    high, low = row_first_call(grid.reshape(2, blocks, cols, BR, BC), twist)
    first, turned = column_tables(n_gx)
    image = None
    chunks = cols // SUB
    for chunk in range(chunks):
        rows = row_second_call(high, low, second, n_gx, chunk)
        data = lax.all_to_all(rows, "gx", split_axis=0, concat_axis=0, tiled=True)
        image = column_call(data, first, turned, image, chunk, chunks)
    return image.reshape(1, 2, TILE // n_gx, TILE)


def base_table(radix, sign):
    index = jnp.arange(radix, dtype=jnp.int32)
    product = index[:, None] * index[None, :] % radix
    angle = sign * 2.0 * math.pi / radix * product.astype(jnp.float32)
    return (jnp.cos(angle), jnp.sin(angle))


def twist_table(radix, sign):
    index = jnp.arange(radix, dtype=jnp.int32)
    product = index[:, None] * index[None, :]
    angle = sign * 2.0 * math.pi / (radix * radix) * product.astype(jnp.float32)
    return (jnp.cos(angle), jnp.sin(angle))


def complex_einsum(form, table, real_part, imag_part):
    cos_part, sin_part = table

    def product(left, right):
        return jnp.einsum(form, left, right, precision=lax.Precision.HIGH)

    new_real = product(cos_part, real_part) - product(sin_part, imag_part)
    new_imag = product(cos_part, imag_part) + product(sin_part, real_part)
    return (new_real, new_imag)


def fourier(real_part, imag_part, radix, sign, to_front):
    count = real_part.shape[0]
    real_part = real_part.reshape(count, radix, radix)
    imag_part = imag_part.reshape(count, radix, radix)
    table = base_table(radix, sign)
    real_part, imag_part = complex_einsum("ak,rab->rkb", table, real_part, imag_part)
    twist_cos, twist_sin = twist_table(radix, sign)
    twist_cos = twist_cos.T
    twist_sin = twist_sin.T
    turned_real = real_part * twist_cos - imag_part * twist_sin
    turned_imag = real_part * twist_sin + imag_part * twist_cos
    if to_front:
        form = "bj,rkb->jkr"
        shape = (radix * radix, count)
    else:
        form = "bj,rkb->rjk"
        shape = (count, radix * radix)
    out_real, out_imag = complex_einsum(form, table, turned_real, turned_imag)
    return (out_real.reshape(shape) / radix, out_imag.reshape(shape) / radix)


def operands(local):
    stations, pols, spectra, parts, channels = local.shape
    inputs = stations * pols
    nout = channels // AVG
    grouped = local.reshape(inputs, spectra, 2, nout, AVG).transpose(3, 0, 1, 2, 4)
    swapped = jnp.stack([grouped[:, :, :, 1], -grouped[:, :, :, 0]], axis=3)
    left = jnp.stack([grouped, swapped], axis=1).reshape(nout, 2 * inputs, spectra, 2 * AVG)
    right = grouped.reshape(nout, inputs, spectra, 2 * AVG)
    return (left, right)


def gram_all(local):
    left, right = operands(local)
    nout, rows_two, spectra, depth = left.shape
    left = left.reshape(nout, rows_two, spectra * depth)
    right = right.reshape(nout, rows_two // 2, spectra * depth)
    return jnp.einsum("oyk,ork->oyr", left, right, preferred_element_type=jnp.float32)


def pair_fits(gx_count, shape):
    lead, st_dev, pols, spectra, parts, fine = shape
    return (
        lead == 1
        and spectra == 1
        and fine == FRADIX * FRADIX
        and (st_dev * pols) % PACK == 0
        and fine % (gx_count * AVG) == 0
        and TILE // gx_count // BR == PACK
    )


def on_device(voltages, tile_of, cell_of):
    grp_count = lax.axis_size("grp")
    gx_count = lax.axis_size("gx")
    lead, st_dev, pols, spectra, parts, fine = voltages.shape
    if grp_count == 2 and pair_fits(gx_count, voltages.shape):
        return pair_plan(voltages, tile_of, cell_of)
    volts = voltages.reshape(st_dev * pols * spectra, 2, fine).astype(jnp.float32)
    spec_re, spec_im = fourier(volts[:, 0], volts[:, 1], FRADIX, -1.0, False)
    spec = jnp.stack([spec_re, spec_im], axis=1).astype(jnp.bfloat16)
    spec = spec.reshape(st_dev, pols, spectra, 2, fine)
    local = lax.all_to_all(spec, "gx", split_axis=4, concat_axis=0, tiled=True)
    gram = gram_all(local)
    factor = 1.0 / math.sqrt(spectra * AVG)
    out_dev = gram.shape[0]
    inputs = gram.shape[2]
    vis = (gram * factor).astype(jnp.bfloat16).reshape(out_dev, 2, inputs, inputs)
    width = 2 * BR * BC
    shaped = vis.reshape(out_dev, 2, inputs // BR, BR, inputs // BC, BC)
    blocks = shaped.transpose(0, 2, 4, 1, 3, 5).reshape(-1, width)
    count_blocks = blocks.shape[0]
    capacity = max(2, count_blocks // (4 * grp_count))
    slots = grp_count * capacity
    me = lax.axis_index("grp")
    groups = tile_of.shape[0]
    marked = (tile_of[:, None, :] == jnp.arange(grp_count, dtype=jnp.int32)[None, :, None]).astype(
        jnp.int32
    )
    rank_all = jnp.sum((jnp.cumsum(marked, axis=2) - marked) * marked, axis=1)
    my_tiles = lax.dynamic_index_in_dim(tile_of, me, 0, keepdims=False)
    my_rank = lax.dynamic_index_in_dim(rank_all, me, 0, keepdims=False)
    slot_id = jnp.where(my_tiles < 0, -1, my_tiles * capacity + my_rank)
    hits = jnp.arange(slots, dtype=jnp.int32)[:, None] == slot_id[None, :]
    filled = jnp.any(hits, axis=1)
    source = jnp.where(filled, jnp.argmax(hits, axis=1), count_blocks)
    padded = jnp.concatenate([blocks, jnp.zeros((1, width), jnp.bfloat16)], axis=0)
    outgoing = jnp.take(padded, source, axis=0)
    outgoing = outgoing.reshape(grp_count, capacity, width)
    arrived = lax.all_to_all(outgoing, "grp", split_axis=0, concat_axis=0, tiled=True)
    slab = TILE // gx_count
    row_blocks = slab // BR
    col_blocks = TILE // BC
    cells_count = row_blocks * col_blocks
    source_group = jnp.arange(groups, dtype=jnp.int32)[:, None]
    slot_flat = jnp.where(tile_of == me, source_group * capacity + rank_all, -1).reshape(-1)
    cell_flat = cell_of.reshape(-1)
    cell_hit = (jnp.arange(cells_count, dtype=jnp.int32)[:, None] == cell_flat[None, :]).astype(
        jnp.bfloat16
    )
    slot_hit = (jnp.arange(slots, dtype=jnp.int32)[:, None] == slot_flat[None, :]).astype(
        jnp.bfloat16
    )
    place = lax.dot_general(
        cell_hit, slot_hit, (((1,), (1,)), ((), ())), preferred_element_type=jnp.float32
    )
    place = place.astype(jnp.bfloat16)
    grid = jnp.dot(place, arrived.reshape(slots, width), preferred_element_type=jnp.float32)
    grid = (
        grid.reshape(row_blocks, col_blocks, 2, BR, BC)
        .transpose(2, 0, 3, 1, 4)
        .reshape(2, slab, TILE)
    )
    rows_re, rows_im = fourier(grid[0], grid[1], TRADIX, 1.0, True)
    rows = jnp.stack([rows_re, rows_im], axis=0).astype(jnp.bfloat16)
    columns = lax.all_to_all(rows, "gx", split_axis=1, concat_axis=2, tiled=True)
    kx_local = columns.shape[1]
    image_re, image_im = fourier(
        columns[0].astype(jnp.float32), columns[1].astype(jnp.float32), TRADIX, 1.0, False
    )
    image = jnp.stack([image_re, image_im], axis=0).reshape(1, 2, kx_local, TILE)
    return image


def solution(mesh):
    in_specs = (P("grp", "gx", None, None, None, None), P(None, "gx"), P(None, "gx"))
    out_specs = P("grp", None, "gx", None)
    return jax.shard_map(
        on_device, mesh=mesh, in_specs=in_specs, out_specs=out_specs, check_vma=False
    )
```

```python
import functools
import math

import jax
import jax.numpy as jnp
import numpy as np
from jax import lax
from jax.experimental import pallas as pl
from jax.experimental.pallas import tpu as pltpu
from jax.sharding import PartitionSpec as P


FRADIX = 128
AVG = 256
BR = 16
BC = 128
TRADIX = 64
TILE = 4096
SUB = 8
PACK = 16
F32 = jnp.float32
BF16 = jnp.bfloat16


def halves(matrix):
    high = matrix.astype(np.float32).astype(BF16)
    low = (matrix - high.astype(np.float64)).astype(np.float32).astype(BF16)
    return high, low


def complex_table(angle, scale):
    cos, sin = scale * np.cos(angle), scale * np.sin(angle)
    return np.stack([np.stack([cos, -sin]), np.stack([sin, cos])])


def turn(product, period, sign):
    return sign * 2.0 * np.pi / period * (product % period)


def spectra_tables(n_gx, out_dev):
    index = np.arange(FRADIX)
    first = complex_table(turn(np.outer(index, index), FRADIX, -1.0), 1.0 / FRADIX)
    first = first.transpose(0, 2, 3, 1).reshape(2 * FRADIX, 2 * FRADIX)
    high, low = halves(first)
    first = np.concatenate([high, low], axis=1)
    angle = turn(np.outer(index, index), FRADIX * FRADIX, -1.0)
    twist = np.stack([np.cos(angle), np.sin(angle)]).astype(np.float32)
    second = complex_table(turn(np.outer(index, index), FRADIX, -1.0), 1.0)
    low_count = FRADIX // (n_gx * out_dev)
    second = second.reshape(2, 2, n_gx, out_dev, low_count, FRADIX)
    second = second.transpose(3, 2, 0, 4, 1, 5).reshape(2 * FRADIX, 2 * FRADIX)
    high, low = halves(second)
    second = np.concatenate([high, low, high], axis=1)
    return first, twist, second


def row_tables():
    cols = TILE // BC
    k1, w = np.arange(cols), np.arange(BC)
    angle = turn(np.outer(k1, w), TILE, 1.0)
    twist = np.stack([np.cos(angle), np.sin(angle)]).astype(np.float32)
    second = complex_table(turn(np.outer(w, w), BC, 1.0), 1.0 / math.sqrt(TILE))
    second = second.transpose(2, 0, 1, 3).reshape(2 * BC, 2 * BC)
    return twist, halves(second)[0]


def column_tables(n_gx):
    count = TILE // BR
    blocks = count // n_gx
    index = np.arange(count)
    first = complex_table(turn(np.outer(index, index), count, 1.0), 1.0 / math.sqrt(TILE))
    first = first.reshape(2, 2, n_gx, blocks, count)
    first = first.transpose(2, 1, 3, 0, 4).reshape(2 * count, 2 * count)
    angle = turn(np.outer(np.arange(BR), index), TILE, 1.0)
    twist = np.stack([np.cos(angle), np.sin(angle)]).astype(np.float32)
    return halves(first)[0], twist


def times(value, factor):
    re, im = value
    c, s = factor
    return (re * c - im * s, re * s + im * c)


def fixed_turn(value, step, count, sign):
    re, im = value
    step = step % count
    if step == 0:
        return value
    if 4 * step == count:
        return (-im, re) if sign > 0 else (im, -re)
    angle = sign * 2.0 * math.pi * step / count
    c, s = math.cos(angle), math.sin(angle)
    if 8 * step == count:
        return ((re - im) * c, (re + im) * c) if sign > 0 else ((re + im) * c, (im - re) * c)
    if 8 * step == 3 * count:
        h = abs(c)
        return ((-re - im) * h, (re - im) * h) if sign > 0 else ((im - re) * h, (-re - im) * h)
    return (re * c - im * s, re * s + im * c)


def butterflies(values, sign):
    count = len(values)
    if count == 1:
        return values
    even = butterflies(values[0::2], sign)
    odd = butterflies(values[1::2], sign)
    out = [None] * count
    for k in range(count // 2):
        turned = fixed_turn(odd[k], k, count, sign)
        out[k] = (even[k][0] + turned[0], even[k][1] + turned[1])
        out[k + count // 2] = (even[k][0] - turned[0], even[k][1] - turned[1])
    return out


def split_value(value):
    high = value.astype(BF16)
    return high, (value - high.astype(F32)).astype(BF16)


def dot_nt(left, right):
    return lax.dot_general(left, right, (((1,), (1,)), ((), ())), preferred_element_type=F32)


def dot_tn(left, right):
    return lax.dot_general(left, right, (((0,), (0,)), ((), ())), preferred_element_type=F32)


def channel_rows(n_gx, scratch, out_ref):
    stride = scratch.shape[0] // PACK
    per = out_ref.shape[2] // FRADIX
    for d in range(n_gx):
        for t in range(per):
            piece = scratch[pl.ds(d * per + t, PACK, stride=stride), :]
            out_ref[d, :, t * FRADIX : (t + 1) * FRADIX] = piece.astype(BF16)


def second_stage(pair, high_ref, low_ref, second_ref, scratch):
    rows = second_ref.shape[0]
    stride = scratch.shape[0] // PACK
    two = 2 * FRADIX
    high = high_ref[2 * pair : 2 * pair + 2].reshape(two, two)
    low = low_ref[2 * pair : 2 * pair + 2].reshape(two, two)
    z = dot_nt(second_ref[...], jnp.concatenate([high, high, low], axis=1))
    scratch[2 * pair * stride : 2 * pair * stride + rows, :] = z[:, :FRADIX]
    scratch[(2 * pair + 1) * stride : (2 * pair + 1) * stride + rows, :] = z[:, FRADIX:]


def spectra_first_kernel(n_gx, v_ref, first_ref, twist_ref, second_ref, high_ref, low_ref, out_ref, scratch):
    for pair in range(PACK // 2):
        v = jnp.concatenate([v_ref[2 * pair], v_ref[2 * pair + 1]], axis=1)
        y = jnp.dot(first_ref[...], jnp.concatenate([v, v], axis=0), preferred_element_type=F32)
        for u in range(2):
            lane = slice(u * FRADIX, (u + 1) * FRADIX)
            re, im = times((y[:FRADIX, lane], y[FRADIX:, lane]), (twist_ref[0], twist_ref[1]))
            for part, value in enumerate((re, im)):
                high, low = split_value(value)
                high_ref[2 * pair + u, :, part * FRADIX : (part + 1) * FRADIX] = high
                low_ref[2 * pair + u, :, part * FRADIX : (part + 1) * FRADIX] = low
    for pair in range(PACK // 2):
        second_stage(pair, high_ref, low_ref, second_ref, scratch)
    channel_rows(n_gx, scratch, out_ref)


def spectra_second_kernel(n_gx, high_ref, low_ref, second_ref, out_ref, scratch):
    for pair in range(PACK // 2):
        second_stage(pair, high_ref, low_ref, second_ref, scratch)
    channel_rows(n_gx, scratch, out_ref)


def whole(x):
    return pl.BlockSpec(x.shape, lambda *i: (0,) * x.ndim)


def spectra_first_call(volts, n_gx, out_dev):
    inputs = volts.shape[0]
    first, twist, second = spectra_tables(n_gx, out_dev)
    rows = 2 * FRADIX // out_dev
    second = second[:rows]
    depth = 2 * AVG
    turned = jax.ShapeDtypeStruct((inputs, FRADIX, 2 * FRADIX), BF16)
    turned_spec = pl.BlockSpec((PACK, FRADIX, 2 * FRADIX), lambda i: (i, 0, 0))
    return pl.pallas_call(
        functools.partial(spectra_first_kernel, n_gx),
        grid=(inputs // PACK,),
        in_specs=[
            pl.BlockSpec((PACK, 2 * FRADIX, FRADIX), lambda i: (i, 0, 0)),
            whole(first),
            whole(twist),
            whole(second),
        ],
        out_specs=[turned_spec, turned_spec, pl.BlockSpec((n_gx, PACK, depth), lambda i: (0, i, 0))],
        out_shape=[turned, turned, jax.ShapeDtypeStruct((n_gx, inputs, depth), BF16)],
        scratch_shapes=[pltpu.VMEM((PACK * (rows + SUB), FRADIX), F32)],
        name="spectra_first",
    )(volts, first, twist, second)


def spectra_second_call(high, low, n_gx, out_dev, o):
    inputs = high.shape[0]
    rows = 2 * FRADIX // out_dev
    second = spectra_tables(n_gx, out_dev)[2][o * rows : (o + 1) * rows]
    depth = 2 * AVG
    turned_spec = pl.BlockSpec((PACK, FRADIX, 2 * FRADIX), lambda i: (i, 0, 0))
    return pl.pallas_call(
        functools.partial(spectra_second_kernel, n_gx),
        grid=(inputs // PACK,),
        in_specs=[turned_spec, turned_spec, whole(second)],
        out_specs=pl.BlockSpec((n_gx, PACK, depth), lambda i: (0, i, 0)),
        out_shape=jax.ShapeDtypeStruct((n_gx, inputs, depth), BF16),
        scratch_shapes=[pltpu.VMEM((PACK * (rows + SUB), FRADIX), F32)],
        name="spectra_second",
    )(high, low, second)


def correlate(x_ref, vis, factor):
    nin, depth = x_ref.shape
    half = depth // 2
    panel = 2 * BC

    def one(p, carry):
        base = pl.multiple_of(p * panel, panel)
        x = x_ref[pl.ds(base, panel), :]
        swapped = jnp.concatenate([x[:, half:], -x[:, :half]], axis=1)
        left = jnp.concatenate([x, swapped], axis=0)
        gram = (dot_nt(left, x_ref[...]) * factor).astype(BF16)
        for e in range(nin // BC):
            vis[0, e, pl.ds(base, panel), :] = gram[:panel, e * BC : (e + 1) * BC]
            vis[1, e, pl.ds(base, panel), :] = gram[panel:, e * BC : (e + 1) * BC]
        return carry

    lax.fori_loop(0, nin // panel, one, 0)


def place_blocks(which, count_ref, list_ref, vis, grid):
    cells = grid.shape[1]
    wide = vis.shape[1]

    def place(s, carry):
        code = list_ref[which, s]
        cell = lax.rem(code, cells)
        block = lax.div(code, cells)
        e = lax.rem(block, wide)
        row = pl.multiple_of(lax.div(block, wide) * BR, BR)
        for part in range(2):
            grid[part, cell] += vis[part, e, pl.ds(row, BR), :].astype(F32)
        return carry

    lax.fori_loop(0, count_ref[which], place, 0)


def gram_kernel(streams, first_call, factor, count_ref, list_ref, *rest):
    x_refs, rest = rest[:streams], rest[streams:]
    out_ref, vis, grid, sem = rest[-4:]
    cells = grid.shape[1]
    if first_call:
        def clear(i, carry):
            grid[:, pl.ds(i * SUB, SUB)] = jnp.zeros((2, SUB, BR, BC), F32)
            return carry

        lax.fori_loop(0, cells // SUB, clear, 0)
    else:
        load = pltpu.make_async_copy(rest[0], grid, sem)
        load.start()
    for which, x_ref in enumerate(x_refs):
        correlate(x_ref, vis, factor)
        if which == 0 and not first_call:
            load.wait()
        place_blocks(which, count_ref, list_ref, vis, grid)
    store = pltpu.make_async_copy(grid, out_ref, sem)
    store.start()
    store.wait()


def gram_call(counts, lists, streams, grid, cells, factor):
    first_call = grid is None
    shape = (2, cells, BR, BC)
    nin, depth = streams[0].shape
    any_spec = pl.BlockSpec(memory_space=pl.ANY)
    vmem = pl.BlockSpec(memory_space=pltpu.VMEM)
    smem = pl.BlockSpec(memory_space=pltpu.SMEM)
    args = (counts, lists) + tuple(streams) + (() if first_call else (grid,))
    flops = len(streams) * 4 * nin * nin * depth
    return pl.pallas_call(
        functools.partial(gram_kernel, len(streams), first_call, factor),
        in_specs=[smem, smem] + [vmem] * len(streams) + ([] if first_call else [any_spec]),
        out_specs=any_spec,
        out_shape=jax.ShapeDtypeStruct(shape, F32),
        scratch_shapes=[
            pltpu.VMEM((2, nin // BC, nin, BC), BF16),
            pltpu.VMEM(shape, F32),
            pltpu.SemaphoreType.DMA,
        ],
        input_output_aliases={} if first_call else {2 + len(streams): 0},
        cost_estimate=pl.CostEstimate(flops=flops, transcendentals=0, bytes_accessed=2**24),
        name="gram",
    )(*args)


def gram_row_kernel(factor, count_ref, list_ref, x_ref, grid_ref, twist_ref, out_ref, vis, grid, scratch, sem):
    cols = TILE // BC
    step = pl.program_id(0)

    @pl.when(step == 0)
    def _():
        load = pltpu.make_async_copy(grid_ref, grid, sem)
        load.start()
        correlate(x_ref, vis, factor)
        load.wait()
        place_blocks(0, count_ref, list_ref, vis, grid)

    for h in range(BR // SUB):
        rows = slice(h * SUB, (h + 1) * SUB)
        values = [(grid[0, step * cols + c, rows], grid[1, step * cols + c, rows]) for c in range(cols)]
        values = butterflies(values, 1.0)
        for k in range(cols):
            factor_k = (twist_ref[0, k : k + 1, :], twist_ref[1, k : k + 1, :])
            re, im = times(values[k], factor_k)
            at = slice(k * BR + h * SUB, k * BR + (h + 1) * SUB)
            scratch[at, :BC] = re
            scratch[at, BC:] = im
    out_ref[0] = scratch[...].astype(BF16)


def gram_row_call(counts, lists, stream, grid, cells, factor, twist):
    nin, _ = stream.shape
    cols = TILE // BC
    blocks = cells // cols
    smem = pl.BlockSpec(memory_space=pltpu.SMEM)
    return pl.pallas_call(
        functools.partial(gram_row_kernel, factor),
        grid=(blocks,),
        in_specs=[
            smem,
            smem,
            pl.BlockSpec(memory_space=pltpu.VMEM),
            pl.BlockSpec(memory_space=pl.ANY),
            whole(twist),
        ],
        out_specs=pl.BlockSpec((1, cols * BR, 2 * BC), lambda i: (i, 0, 0)),
        out_shape=jax.ShapeDtypeStruct((blocks, cols * BR, 2 * BC), BF16),
        scratch_shapes=[
            pltpu.VMEM((2, nin // BC, nin, BC), BF16),
            pltpu.VMEM((2, cells, BR, BC), F32),
            pltpu.VMEM((cols * BR, 2 * BC), F32),
            pltpu.SemaphoreType.DMA,
        ],
        name="gram_row",
    )(counts, lists, stream, grid, twist)


def row_second_kernel(data_ref, second_ref, out_ref, scratch):
    blocks = data_ref.shape[0]
    lanes = SUB * BR
    rows = 2 * BC
    stride = scratch.shape[0] // blocks
    for b in range(blocks // 2):
        data = data_ref[2 * b : 2 * b + 2].reshape(2 * lanes, rows)
        z = dot_nt(second_ref[...], data)
        for u in range(2):
            at = (2 * b + u) * stride
            scratch[at : at + rows, :] = z[:, u * lanes : (u + 1) * lanes]
    n_gx, lows, _, _ = out_ref.shape
    for d in range(n_gx):
        for k in range(lows):
            for part in range(2):
                row = (d * lows + k) * 2 + part
                piece = scratch[pl.ds(row, blocks, stride=stride), :]
                out_ref[d, k, part * blocks : (part + 1) * blocks, :] = piece.astype(BF16)


def row_second_call(data, second, n_gx, start, count):
    blocks = data.shape[0]
    lanes = SUB * BR
    lows = BC // n_gx
    return pl.pallas_call(
        row_second_kernel,
        grid=(count,),
        in_specs=[
            pl.BlockSpec((blocks, lanes, 2 * BC), lambda i: (0, start + i, 0)),
            whole(second),
        ],
        out_specs=pl.BlockSpec((n_gx, lows, 2 * blocks, lanes), lambda i: (0, 0, 0, i)),
        out_shape=jax.ShapeDtypeStruct((n_gx, lows, 2 * blocks, count * lanes), BF16),
        scratch_shapes=[pltpu.VMEM((blocks * (2 * BC + SUB), lanes), F32)],
        cost_estimate=pl.CostEstimate(flops=2**31, transcendentals=0, bytes_accessed=2**22),
        name="row_second",
    )(data, second)


COLUMN_STEP = 2


def column_kernel(data_ref, first_ref, twist_ref, *rest):
    out_ref, scratch = rest[-2], rest[-1]
    n_gx, _, rows, lanes = data_ref.shape
    count = TILE // BR
    span = scratch.shape[0] // COLUMN_STEP
    for q in range(COLUMN_STEP):
        data = data_ref[:, q].reshape(n_gx * rows, lanes)
        mixed = dot_tn(data, first_ref[...])
        for b in range(2 * count // BC):
            scratch[q * span + b * lanes : q * span + (b + 1) * lanes, :] = mixed[:, b * BC : (b + 1) * BC]
    for q in range(COLUMN_STEP):
        for b in range(count // BC):
            lane = slice(b * BC, (b + 1) * BC)
            values = []
            for r in range(BR):
                value = (
                    scratch[pl.ds(q * span + b * lanes + r, SUB, stride=BR), :],
                    scratch[pl.ds(q * span + (count // BC + b) * lanes + r, SUB, stride=BR), :],
                )
                factor = (twist_ref[0, r : r + 1, lane], twist_ref[1, r : r + 1, lane])
                values.append(times(value, factor) if r else value)
            values = butterflies(values, 1.0)
            for k in range(BR):
                at = slice(k * count + b * BC, k * count + (b + 1) * BC)
                out_ref[0, q, 0, :, at] = values[k][0]
                out_ref[1, q, 0, :, at] = values[k][1]


def column_call(data, first, twist, image, part, chunk, chunks):
    n_gx, lows, rows, _ = data.shape
    lanes = SUB * BR
    alias = image is not None
    shape = (2, lows, chunks, SUB, TILE)
    return pl.pallas_call(
        column_kernel,
        grid=(lows // COLUMN_STEP,),
        in_specs=[
            pl.BlockSpec((n_gx, COLUMN_STEP, rows, lanes), lambda i: (0, i, 0, part)),
            whole(first),
            whole(twist),
        ]
        + ([pl.BlockSpec(memory_space=pl.ANY)] if alias else []),
        out_specs=pl.BlockSpec((2, COLUMN_STEP, 1, SUB, TILE), lambda i: (0, i, chunk, 0, 0)),
        out_shape=jax.ShapeDtypeStruct(shape, F32),
        scratch_shapes=[pltpu.VMEM((COLUMN_STEP * 2 * (TILE // BR) // BC * lanes, BC), F32)],
        input_output_aliases={3: 0} if alias else {},
        cost_estimate=pl.CostEstimate(flops=2**30, transcendentals=0, bytes_accessed=2**22),
        name="column",
    )(data, first, twist, *((image,) if alias else ()))


def work_lists(tile_of, cell_of, me, out_dev, cells):
    groups, blocks = tile_of.shape
    per = blocks // out_dev
    taken = (tile_of == me).reshape(groups, out_dev, per)
    number = taken.astype(jnp.int32)
    rank = jnp.cumsum(number, axis=2) - number
    slot = jnp.where(taken, rank, -1)
    code = jnp.arange(per, dtype=jnp.int32) * cells + cell_of.reshape(groups, out_dev, per)
    hit = jnp.arange(per, dtype=jnp.int32)[:, None] == slot[:, :, None, :]
    lists = jnp.sum(jnp.where(hit, code[:, :, None, :], 0), axis=3)
    return jnp.sum(number, axis=2), lists


def row_chunks(groups):
    return (1,) * groups


def pair_plan(voltages, tile_of, cell_of):
    n_gx = lax.axis_size("gx")
    _, st_dev, pols, spectra, _, fine = voltages.shape
    inputs = st_dev * pols
    out_dev = fine // (n_gx * AVG)
    cells = (TILE // n_gx // BR) * (TILE // BC)
    cols = TILE // BC
    me = lax.axis_index("grp")
    counts, lists = work_lists(tile_of, cell_of, me, out_dev, cells)
    swap = jnp.where(me == 0, jnp.arange(2), jnp.arange(2)[::-1])
    counts, lists = jnp.take(counts, swap, axis=0), jnp.take(lists, swap, axis=0)

    volts = voltages.reshape(inputs, 2, FRADIX, FRADIX).transpose(0, 2, 1, 3)
    volts = volts.reshape(inputs, 2 * FRADIX, FRADIX)
    factor = 1.0 / math.sqrt(spectra * AVG)
    high, low, spec = spectra_first_call(volts, n_gx, out_dev)
    grid = None
    for o in range(out_dev):
        if o:
            spec = spectra_second_call(high, low, n_gx, out_dev, o)
        mine = lax.all_to_all(spec, "gx", split_axis=0, concat_axis=0, tiled=True)
        mine = mine.reshape(n_gx * inputs, 2 * AVG)
        number, list_of = counts[0, o : o + 1], lists[0, o : o + 1]
        if o:
            number = jnp.concatenate([number, counts[1, o - 1 : o]])
            list_of = jnp.concatenate([list_of, lists[1, o - 1 : o]])
        streams = (mine, other) if o else (mine,)
        grid = gram_call(number, list_of, streams, grid, cells, factor)
        other = lax.ppermute(mine, "grp", [(0, 1), (1, 0)])
    twist, second = row_tables()
    last = out_dev - 1
    mixed = gram_row_call(counts[1, last:], lists[1, last:], other, grid, cells, factor, twist)
    first, turned = column_tables(n_gx)
    image = None
    start = 0
    groups = cols // SUB
    for size in row_chunks(groups):
        rows = row_second_call(mixed, second, n_gx, start, size)
        data = lax.all_to_all(rows, "gx", split_axis=0, concat_axis=0, tiled=True)
        for part in range(size):
            image = column_call(data, first, turned, image, part, start + part, groups)
        start += size
    return image.reshape(1, 2, TILE // n_gx, TILE)


def base_table(radix, sign):
    index = jnp.arange(radix, dtype=jnp.int32)
    product = index[:, None] * index[None, :] % radix
    angle = sign * 2.0 * math.pi / radix * product.astype(jnp.float32)
    return (jnp.cos(angle), jnp.sin(angle))


def twist_table(radix, sign):
    index = jnp.arange(radix, dtype=jnp.int32)
    product = index[:, None] * index[None, :]
    angle = sign * 2.0 * math.pi / (radix * radix) * product.astype(jnp.float32)
    return (jnp.cos(angle), jnp.sin(angle))


def complex_einsum(form, table, real_part, imag_part):
    cos_part, sin_part = table

    def product(left, right):
        return jnp.einsum(form, left, right, precision=lax.Precision.HIGH)

    new_real = product(cos_part, real_part) - product(sin_part, imag_part)
    new_imag = product(cos_part, imag_part) + product(sin_part, real_part)
    return (new_real, new_imag)


def fourier(real_part, imag_part, radix, sign, to_front):
    count = real_part.shape[0]
    real_part = real_part.reshape(count, radix, radix)
    imag_part = imag_part.reshape(count, radix, radix)
    table = base_table(radix, sign)
    real_part, imag_part = complex_einsum("ak,rab->rkb", table, real_part, imag_part)
    twist_cos, twist_sin = twist_table(radix, sign)
    twist_cos = twist_cos.T
    twist_sin = twist_sin.T
    turned_real = real_part * twist_cos - imag_part * twist_sin
    turned_imag = real_part * twist_sin + imag_part * twist_cos
    if to_front:
        form = "bj,rkb->jkr"
        shape = (radix * radix, count)
    else:
        form = "bj,rkb->rjk"
        shape = (count, radix * radix)
    out_real, out_imag = complex_einsum(form, table, turned_real, turned_imag)
    return (out_real.reshape(shape) / radix, out_imag.reshape(shape) / radix)


def operands(local):
    stations, pols, spectra, _, channels = local.shape
    inputs = stations * pols
    nout = channels // AVG
    grouped = local.reshape(inputs, spectra, 2, nout, AVG).transpose(3, 0, 1, 2, 4)
    swapped = jnp.stack([grouped[:, :, :, 1], -grouped[:, :, :, 0]], axis=3)
    left = jnp.stack([grouped, swapped], axis=1).reshape(nout, 2 * inputs, spectra, 2 * AVG)
    right = grouped.reshape(nout, inputs, spectra, 2 * AVG)
    return (left, right)


def gram_all(local):
    left, right = operands(local)
    nout, rows_two, spectra, depth = left.shape
    left = left.reshape(nout, rows_two, spectra * depth)
    right = right.reshape(nout, rows_two // 2, spectra * depth)
    return jnp.einsum("oyk,ork->oyr", left, right, preferred_element_type=jnp.float32)


def pair_fits(gx_count, shape):
    lead, st_dev, pols, spectra, _, fine = shape
    return (
        lead == 1
        and spectra == 1
        and fine == FRADIX * FRADIX
        and (st_dev * pols) % PACK == 0
        and fine % (gx_count * AVG) == 0
        and TILE // gx_count // BR == PACK
    )


def on_device(voltages, tile_of, cell_of):
    grp_count = lax.axis_size("grp")
    gx_count = lax.axis_size("gx")
    _, st_dev, pols, spectra, _, fine = voltages.shape
    if grp_count == 2 and pair_fits(gx_count, voltages.shape):
        return pair_plan(voltages, tile_of, cell_of)
    volts = voltages.reshape(st_dev * pols * spectra, 2, fine).astype(jnp.float32)
    spec_re, spec_im = fourier(volts[:, 0], volts[:, 1], FRADIX, -1.0, False)
    spec = jnp.stack([spec_re, spec_im], axis=1).astype(jnp.bfloat16)
    spec = spec.reshape(st_dev, pols, spectra, 2, fine)
    local = lax.all_to_all(spec, "gx", split_axis=4, concat_axis=0, tiled=True)
    gram = gram_all(local)
    factor = 1.0 / math.sqrt(spectra * AVG)
    out_dev = gram.shape[0]
    inputs = gram.shape[2]
    vis = (gram * factor).astype(jnp.bfloat16).reshape(out_dev, 2, inputs, inputs)
    width = 2 * BR * BC
    shaped = vis.reshape(out_dev, 2, inputs // BR, BR, inputs // BC, BC)
    blocks = shaped.transpose(0, 2, 4, 1, 3, 5).reshape(-1, width)
    count_blocks = blocks.shape[0]
    capacity = max(2, count_blocks // (4 * grp_count))
    slots = grp_count * capacity
    me = lax.axis_index("grp")
    groups = tile_of.shape[0]
    marked = (tile_of[:, None, :] == jnp.arange(grp_count, dtype=jnp.int32)[None, :, None]).astype(
        jnp.int32
    )
    rank_all = jnp.sum((jnp.cumsum(marked, axis=2) - marked) * marked, axis=1)
    my_tiles = lax.dynamic_index_in_dim(tile_of, me, 0, keepdims=False)
    my_rank = lax.dynamic_index_in_dim(rank_all, me, 0, keepdims=False)
    slot_id = jnp.where(my_tiles < 0, -1, my_tiles * capacity + my_rank)
    hits = jnp.arange(slots, dtype=jnp.int32)[:, None] == slot_id[None, :]
    filled = jnp.any(hits, axis=1)
    source = jnp.where(filled, jnp.argmax(hits, axis=1), count_blocks)
    padded = jnp.concatenate([blocks, jnp.zeros((1, width), jnp.bfloat16)], axis=0)
    outgoing = jnp.take(padded, source, axis=0)
    outgoing = outgoing.reshape(grp_count, capacity, width)
    arrived = lax.all_to_all(outgoing, "grp", split_axis=0, concat_axis=0, tiled=True)
    slab = TILE // gx_count
    row_blocks = slab // BR
    col_blocks = TILE // BC
    cells_count = row_blocks * col_blocks
    source_group = jnp.arange(groups, dtype=jnp.int32)[:, None]
    slot_flat = jnp.where(tile_of == me, source_group * capacity + rank_all, -1).reshape(-1)
    cell_flat = cell_of.reshape(-1)
    cell_hit = (jnp.arange(cells_count, dtype=jnp.int32)[:, None] == cell_flat[None, :]).astype(
        jnp.bfloat16
    )
    slot_hit = (jnp.arange(slots, dtype=jnp.int32)[:, None] == slot_flat[None, :]).astype(
        jnp.bfloat16
    )
    place = lax.dot_general(
        cell_hit, slot_hit, (((1,), (1,)), ((), ())), preferred_element_type=jnp.float32
    )
    place = place.astype(jnp.bfloat16)
    grid = jnp.dot(place, arrived.reshape(slots, width), preferred_element_type=jnp.float32)
    grid = (
        grid.reshape(row_blocks, col_blocks, 2, BR, BC)
        .transpose(2, 0, 3, 1, 4)
        .reshape(2, slab, TILE)
    )
    rows_re, rows_im = fourier(grid[0], grid[1], TRADIX, 1.0, True)
    rows = jnp.stack([rows_re, rows_im], axis=0).astype(jnp.bfloat16)
    columns = lax.all_to_all(rows, "gx", split_axis=1, concat_axis=2, tiled=True)
    kx_local = columns.shape[1]
    image_re, image_im = fourier(
        columns[0].astype(jnp.float32), columns[1].astype(jnp.float32), TRADIX, 1.0, False
    )
    image = jnp.stack([image_re, image_im], axis=0).reshape(1, 2, kx_local, TILE)
    return image


def solution(mesh):
    in_specs = (P("grp", "gx", None, None, None, None), P(None, "gx"), P(None, "gx"))
    out_specs = P("grp", None, "gx", None)
    return jax.shard_map(
        on_device, mesh=mesh, in_specs=in_specs, out_specs=out_specs, check_vma=False
    )
```

```python
import functools
import math

import jax
import jax.numpy as jnp
import numpy as np
from jax import lax
from jax.experimental import pallas as pl
from jax.experimental.pallas import tpu as pltpu
from jax.sharding import PartitionSpec as P


FRADIX = 128
AVG = 256
BR = 16
BC = 128
TRADIX = 64
TILE = 4096
SUB = 8
PACK = 16
F32 = jnp.float32
BF16 = jnp.bfloat16


def halves(matrix):
    high = matrix.astype(np.float32).astype(BF16)
    low = (matrix - high.astype(np.float64)).astype(np.float32).astype(BF16)
    return high, low


def complex_table(angle, scale):
    cos, sin = scale * np.cos(angle), scale * np.sin(angle)
    return np.stack([np.stack([cos, -sin]), np.stack([sin, cos])])


def turn(product, period, sign):
    return sign * 2.0 * np.pi / period * (product % period)


def spectra_tables(n_gx, out_dev):
    index = np.arange(FRADIX)
    first = complex_table(turn(np.outer(index, index), FRADIX, -1.0), 1.0 / FRADIX)
    first = first.transpose(0, 2, 3, 1).reshape(2 * FRADIX, 2 * FRADIX)
    high, low = halves(first)
    first = np.concatenate([high, low], axis=1)
    angle = turn(np.outer(index, index), FRADIX * FRADIX, -1.0)
    twist = np.stack([np.cos(angle), np.sin(angle)]).astype(np.float32)
    second = complex_table(turn(np.outer(index, index), FRADIX, -1.0), 1.0)
    low_count = FRADIX // (n_gx * out_dev)
    second = second.reshape(2, 2, n_gx, out_dev, low_count, FRADIX)
    second = second.transpose(3, 2, 0, 4, 1, 5).reshape(2 * FRADIX, 2 * FRADIX)
    high, low = halves(second)
    second = np.concatenate([high, low, high], axis=1)
    return first, twist, second


def row_tables():
    cols = TILE // BC
    k1, w = np.arange(cols), np.arange(BC)
    angle = turn(np.outer(k1, w), TILE, 1.0)
    twist = np.stack([np.cos(angle), np.sin(angle)]).astype(np.float32)
    second = complex_table(turn(np.outer(w, w), BC, 1.0), 1.0 / math.sqrt(TILE))
    second = second.transpose(2, 0, 1, 3).reshape(2 * BC, 2 * BC)
    return twist, halves(second)[0]


def column_tables(n_gx):
    count = TILE // BR
    blocks = count // n_gx
    index = np.arange(count)
    first = complex_table(turn(np.outer(index, index), count, 1.0), 1.0 / math.sqrt(TILE))
    first = first.reshape(2, 2, n_gx, blocks, count)
    first = first.transpose(2, 1, 3, 0, 4).reshape(2 * count, 2 * count)
    return halves(first)[0]


def column_twist():
    shape = (BR, TILE // BR)
    product = lax.broadcasted_iota(jnp.int32, shape, 0) * lax.broadcasted_iota(jnp.int32, shape, 1)
    angle = 2.0 * math.pi / TILE * product.astype(F32)
    return jnp.cos(angle), jnp.sin(angle)


def times(value, factor):
    re, im = value
    c, s = factor
    return (re * c - im * s, re * s + im * c)


def fixed_turn(value, step, count, sign):
    re, im = value
    step = step % count
    if step == 0:
        return value
    if 4 * step == count:
        return (-im, re) if sign > 0 else (im, -re)
    angle = sign * 2.0 * math.pi * step / count
    c, s = math.cos(angle), math.sin(angle)
    if 8 * step == count:
        return ((re - im) * c, (re + im) * c) if sign > 0 else ((re + im) * c, (im - re) * c)
    if 8 * step == 3 * count:
        h = abs(c)
        return ((-re - im) * h, (re - im) * h) if sign > 0 else ((im - re) * h, (-re - im) * h)
    return (re * c - im * s, re * s + im * c)


def butterflies(values, sign):
    count = len(values)
    if count == 1:
        return values
    even = butterflies(values[0::2], sign)
    odd = butterflies(values[1::2], sign)
    out = [None] * count
    for k in range(count // 2):
        turned = fixed_turn(odd[k], k, count, sign)
        out[k] = (even[k][0] + turned[0], even[k][1] + turned[1])
        out[k + count // 2] = (even[k][0] - turned[0], even[k][1] - turned[1])
    return out


def split_value(value):
    high = value.astype(BF16)
    return high, (value - high.astype(F32)).astype(BF16)


def dot_nt(left, right):
    return lax.dot_general(left, right, (((1,), (1,)), ((), ())), preferred_element_type=F32)


def dot_tn(left, right):
    return lax.dot_general(left, right, (((0,), (0,)), ((), ())), preferred_element_type=F32)


def channel_rows(n_gx, scratch, out_ref):
    stride = scratch.shape[0] // PACK
    channels = out_ref.shape[1]
    per = out_ref.shape[3] // FRADIX
    for o in range(channels):
        for d in range(n_gx):
            for t in range(per):
                piece = scratch[pl.ds((o * n_gx + d) * per + t, PACK, stride=stride), :]
                out_ref[d, o, :, t * FRADIX : (t + 1) * FRADIX] = piece.astype(BF16)


def second_stage(pair, high_ref, low_ref, second_ref, scratch):
    rows = second_ref.shape[0]
    stride = scratch.shape[0] // PACK
    two = 2 * FRADIX
    high = high_ref[2 * pair : 2 * pair + 2].reshape(two, two)
    low = low_ref[2 * pair : 2 * pair + 2].reshape(two, two)
    z = dot_nt(second_ref[...], jnp.concatenate([high, high, low], axis=1))
    scratch[2 * pair * stride : 2 * pair * stride + rows, :] = z[:, :FRADIX]
    scratch[(2 * pair + 1) * stride : (2 * pair + 1) * stride + rows, :] = z[:, FRADIX:]


def spectra_first_kernel(n_gx, v_ref, first_ref, twist_ref, second_ref, high_ref, low_ref, out_ref, scratch):
    for pair in range(PACK // 2):
        v = jnp.concatenate([v_ref[2 * pair], v_ref[2 * pair + 1]], axis=1)
        y = jnp.dot(first_ref[...], jnp.concatenate([v, v], axis=0), preferred_element_type=F32)
        for u in range(2):
            lane = slice(u * FRADIX, (u + 1) * FRADIX)
            re, im = times((y[:FRADIX, lane], y[FRADIX:, lane]), (twist_ref[0], twist_ref[1]))
            for part, value in enumerate((re, im)):
                high, low = split_value(value)
                high_ref[2 * pair + u, :, part * FRADIX : (part + 1) * FRADIX] = high
                low_ref[2 * pair + u, :, part * FRADIX : (part + 1) * FRADIX] = low
    for pair in range(PACK // 2):
        second_stage(pair, high_ref, low_ref, second_ref, scratch)
    channel_rows(n_gx, scratch, out_ref)


def spectra_second_kernel(n_gx, high_ref, low_ref, second_ref, out_ref, scratch):
    for pair in range(PACK // 2):
        second_stage(pair, high_ref, low_ref, second_ref, scratch)
    channel_rows(n_gx, scratch, out_ref)


def whole(x):
    return pl.BlockSpec(x.shape, lambda *i: (0,) * x.ndim)


def spectra_call(volts, turned, tables, n_gx, out_dev, start, stop):
    first, twist, second = tables
    per = 2 * FRADIX // out_dev
    second = second[start * per : stop * per]
    depth = 2 * AVG
    channels = stop - start
    lead = volts if turned is None else turned[0]
    inputs = lead.shape[0]
    turned_shape = jax.ShapeDtypeStruct((inputs, FRADIX, 2 * FRADIX), BF16)
    turned_spec = pl.BlockSpec((PACK, FRADIX, 2 * FRADIX), lambda i: (i, 0, 0))
    out_spec = pl.BlockSpec((n_gx, channels, PACK, depth), lambda i: (0, 0, i, 0))
    out_shape = jax.ShapeDtypeStruct((n_gx, channels, inputs, depth), BF16)
    scratch = [pltpu.VMEM((PACK * (channels * per + SUB), FRADIX), F32)]
    if turned is None:
        return pl.pallas_call(
            functools.partial(spectra_first_kernel, n_gx),
            grid=(inputs // PACK,),
            in_specs=[
                pl.BlockSpec((PACK, 2 * FRADIX, FRADIX), lambda i: (i, 0, 0)),
                whole(first),
                whole(twist),
                whole(second),
            ],
            out_specs=[turned_spec, turned_spec, out_spec],
            out_shape=[turned_shape, turned_shape, out_shape],
            scratch_shapes=scratch,
            name="spectra_first",
        )(volts, first, twist, second)
    return pl.pallas_call(
        functools.partial(spectra_second_kernel, n_gx),
        grid=(inputs // PACK,),
        in_specs=[turned_spec, turned_spec, whole(second)],
        out_specs=out_spec,
        out_shape=out_shape,
        scratch_shapes=scratch,
        name="spectra_second",
    )(*turned, second)


def correlate(x_ref, slot, vis, factor):
    sources, _, inputs, depth = x_ref.shape
    nin = sources * inputs
    half = depth // 2
    group = sources // 4
    panel = group * inputs

    def one(p, carry):
        base = pl.multiple_of(p * panel, panel)
        x = x_ref[pl.ds(p * group, group), slot].reshape(panel, depth)
        swapped = jnp.concatenate([x[:, half:], -x[:, :half]], axis=1)
        left = jnp.concatenate([x, swapped], axis=0)
        right = x_ref[:, slot].reshape(nin, depth)
        gram = (dot_nt(left, right) * factor).astype(BF16)
        for e in range(nin // BC):
            vis[0, e, pl.ds(base, panel), :] = gram[:panel, e * BC : (e + 1) * BC]
            vis[1, e, pl.ds(base, panel), :] = gram[panel:, e * BC : (e + 1) * BC]
        return carry

    lax.fori_loop(0, sources // group, one, 0)


def place_blocks(which, count_ref, list_ref, vis, grid):
    cells = grid.shape[1]
    wide = vis.shape[1]

    def place(s, carry):
        code = list_ref[which, s]
        cell = lax.rem(code, cells)
        block = lax.div(code, cells)
        e = lax.rem(block, wide)
        row = pl.multiple_of(lax.div(block, wide) * BR, BR)
        for part in range(2):
            grid[part, cell] += vis[part, e, pl.ds(row, BR), :].astype(F32)
        return carry

    lax.fori_loop(0, count_ref[which], place, 0)


LOADS = 8


def split_copies(source, target, sems):
    share = target.shape[1] // LOADS
    copies = []
    for i in range(LOADS):
        at = pl.ds(i * share, share)
        copies.append(pltpu.make_async_copy(source.at[:, at], target.at[:, at], sems.at[i]))
    return copies


def gram_kernel(slots, first_call, factor, count_ref, list_ref, *rest):
    x_refs, rest = rest[: len(slots)], rest[len(slots) :]
    out_ref, vis, grid, sems = rest[-4:]
    cells = grid.shape[1]
    if first_call:

        def clear(i, carry):
            grid[:, pl.ds(i * SUB, SUB)] = jnp.zeros((2, SUB, BR, BC), F32)
            return carry

        lax.fori_loop(0, cells // SUB, clear, 0)
    else:
        loads = split_copies(rest[0], grid, sems)
        for load in loads:
            load.start()
    which = 0
    for x_ref, many in zip(x_refs, slots):
        for slot in range(many):
            correlate(x_ref, slot, vis, factor)
            if which == 0 and not first_call:
                for load in loads:
                    load.wait()
            place_blocks(which, count_ref, list_ref, vis, grid)
            which += 1
    stores = split_copies(grid, out_ref, sems)
    for store in stores:
        store.start()
    for store in stores:
        store.wait()


def gram_call(counts, lists, streams, grid, cells, factor):
    first_call = grid is None
    shape = (2, cells, BR, BC)
    sources, _, inputs, depth = streams[0].shape
    nin = sources * inputs
    slots = tuple(x.shape[1] for x in streams)
    any_spec = pl.BlockSpec(memory_space=pl.ANY)
    vmem = pl.BlockSpec(memory_space=pltpu.VMEM)
    smem = pl.BlockSpec(memory_space=pltpu.SMEM)
    args = (counts, lists) + tuple(streams) + (() if first_call else (grid,))
    flops = sum(slots) * 4 * nin * nin * depth
    return pl.pallas_call(
        functools.partial(gram_kernel, slots, first_call, factor),
        in_specs=[smem, smem] + [vmem] * len(streams) + ([] if first_call else [any_spec]),
        out_specs=any_spec,
        out_shape=jax.ShapeDtypeStruct(shape, F32),
        scratch_shapes=[
            pltpu.VMEM((2, nin // BC, nin, BC), BF16),
            pltpu.VMEM(shape, F32),
            pltpu.SemaphoreType.DMA((LOADS,)),
        ],
        input_output_aliases={} if first_call else {2 + len(streams): 0},
        cost_estimate=pl.CostEstimate(flops=flops, transcendentals=0, bytes_accessed=2**24),
        name="gram",
    )(*args)


def row_block(block, grid, twist_ref, stage, turned):
    cols = TILE // BC
    inner = cols // 4
    for h in range(BR // SUB):
        rows = slice(h * SUB, (h + 1) * SUB)
        for q in range(4):
            at = [block * cols + 4 * m + q for m in range(inner)]
            values = butterflies([(grid[0, c, rows], grid[1, c, rows]) for c in at], 1.0)
            for k in range(inner):
                re, im = fixed_turn(values[k], q * k, cols, 1.0)
                stage[h, 0, q * inner + k] = re
                stage[h, 1, q * inner + k] = im
    for k in range(inner):
        halves_of = []
        for h in range(BR // SUB):
            values = [(stage[h, 0, q * inner + k], stage[h, 1, q * inner + k]) for q in range(4)]
            values = butterflies(values, 1.0)
            for m in range(4):
                at = k + m * inner
                if at:
                    factor = (twist_ref[0, at : at + 1, :], twist_ref[1, at : at + 1, :])
                    values[m] = times(values[m], factor)
            halves_of.append(values)
        for m in range(4):
            at = slice((k + m * inner) * BR, (k + m * inner + 1) * BR)
            for part in range(2):
                both = jnp.concatenate([values[m][part] for values in halves_of], axis=0)
                turned[block, at, part * BC : (part + 1) * BC] = both.astype(BF16)


def rows_kernel(
    factor, count_ref, list_ref, x_ref, grid_ref, twist_ref, second_ref, out_ref, vis, grid, stage, turned, scratch, sems
):
    blocks = turned.shape[0]
    lanes = SUB * BR
    rows = 2 * BC
    step = pl.program_id(0)

    @pl.when(step == 0)
    def _():
        loads = split_copies(grid_ref, grid, sems)
        for load in loads:
            load.start()
        for slot in range(x_ref.shape[1]):
            correlate(x_ref, slot, vis, factor)
            if slot == 0:
                for load in loads:
                    load.wait()
            place_blocks(slot, count_ref, list_ref, vis, grid)

        def one(block, carry):
            row_block(block, grid, twist_ref, stage, turned)
            return carry

        lax.fori_loop(0, blocks, one, 0)

    stride = scratch.shape[0] // blocks
    at_lane = pl.ds(pl.multiple_of(step * lanes, lanes), lanes)
    for b in range(blocks // 2):
        data = turned[2 * b : 2 * b + 2, at_lane].reshape(2 * lanes, rows)
        z = dot_nt(second_ref[...], data)
        for u in range(2):
            at = (2 * b + u) * stride
            scratch[at : at + rows, :] = z[:, u * lanes : (u + 1) * lanes]
    n_gx, lows, _, _ = out_ref.shape
    for d in range(n_gx):
        for k in range(lows):
            for part in range(2):
                row = (d * lows + k) * 2 + part
                piece = scratch[pl.ds(row, blocks, stride=stride), :]
                out_ref[d, k, part * blocks : (part + 1) * blocks, :] = piece.astype(BF16)


def rows_call(counts, lists, stream, grid, cells, factor, twist, second, n_gx):
    sources, _, inputs, _ = stream.shape
    nin = sources * inputs
    cols = TILE // BC
    blocks = cells // cols
    lanes = SUB * BR
    lows = BC // n_gx
    smem = pl.BlockSpec(memory_space=pltpu.SMEM)
    return pl.pallas_call(
        functools.partial(rows_kernel, factor),
        grid=(cols // SUB,),
        in_specs=[
            smem,
            smem,
            whole(stream),
            pl.BlockSpec(memory_space=pl.ANY),
            whole(twist),
            whole(second),
        ],
        out_specs=pl.BlockSpec((n_gx, lows, 2 * blocks, lanes), lambda i: (0, 0, 0, i)),
        out_shape=jax.ShapeDtypeStruct((n_gx, lows, 2 * blocks, cols * BR), BF16),
        scratch_shapes=[
            pltpu.VMEM((2, nin // BC, nin, BC), BF16),
            pltpu.VMEM((2, cells, BR, BC), F32),
            pltpu.VMEM((BR // SUB, 2, cols, SUB, BC), F32),
            pltpu.VMEM((blocks, cols * BR, 2 * BC), BF16),
            pltpu.VMEM((blocks * (2 * BC + SUB), lanes), F32),
            pltpu.SemaphoreType.DMA((LOADS,)),
        ],
        name="rows",
    )(counts, lists, stream, grid, twist, second)


def column_kernel(data_ref, first_ref, cos_ref, sin_ref, out_ref, scratch):
    n_gx, _, rows, lanes = data_ref.shape
    count = TILE // BR
    mixed = dot_tn(data_ref[:, 0].reshape(n_gx * rows, lanes), first_ref[...])
    for b in range(2 * count // BC):
        scratch[b * lanes : (b + 1) * lanes, :] = mixed[:, b * BC : (b + 1) * BC]
    for g in range(lanes // (SUB * BR)):
        for b in range(count // BC):
            lane = slice(b * BC, (b + 1) * BC)
            values = []
            for r in range(BR):
                at = g * SUB * BR + r
                value = (
                    scratch[pl.ds(b * lanes + at, SUB, stride=BR), :],
                    scratch[pl.ds((count // BC + b) * lanes + at, SUB, stride=BR), :],
                )
                factor = (cos_ref[r : r + 1, lane], sin_ref[r : r + 1, lane])
                values.append(times(value, factor) if r else value)
            values = butterflies(values, 1.0)
            for k in range(BR):
                at = slice(k * count + b * BC, k * count + (b + 1) * BC)
                out_ref[0, 0, g * SUB : (g + 1) * SUB, at] = values[k][0]
                out_ref[1, 0, g * SUB : (g + 1) * SUB, at] = values[k][1]


def column_call(data, first, cos, sin):
    n_gx, lows, rows, lanes = data.shape
    cols = TILE // BC
    return pl.pallas_call(
        column_kernel,
        grid=(lows,),
        in_specs=[
            pl.BlockSpec((n_gx, 1, rows, lanes), lambda i: (0, i, 0, 0)),
            whole(first),
            whole(cos),
            whole(sin),
        ],
        out_specs=pl.BlockSpec((2, 1, cols, TILE), lambda i: (0, i, 0, 0)),
        out_shape=jax.ShapeDtypeStruct((2, lows, cols, TILE), F32),
        scratch_shapes=[pltpu.VMEM((2 * (TILE // BR) // BC * lanes, BC), F32)],
        name="column",
    )(data, first, cos, sin)


def work_lists(tile_of, cell_of, me, out_dev, cells):
    groups, blocks = tile_of.shape
    per = blocks // out_dev
    taken = (tile_of == me).reshape(groups, out_dev, per)
    number = taken.astype(jnp.int32)
    rank = jnp.cumsum(number, axis=2) - number
    slot = jnp.where(taken, rank, -1)
    code = jnp.arange(per, dtype=jnp.int32) * cells + cell_of.reshape(groups, out_dev, per)
    hit = jnp.arange(per, dtype=jnp.int32)[:, None] == slot[:, :, None, :]
    lists = jnp.sum(jnp.where(hit, code[:, :, None, :], 0), axis=3)
    return jnp.sum(number, axis=2), lists


def pair_plan(voltages, tile_of, cell_of):
    n_gx = lax.axis_size("gx")
    _, st_dev, pols, spectra, _, fine = voltages.shape
    inputs = st_dev * pols
    out_dev = fine // (n_gx * AVG)
    cells = (TILE // n_gx // BR) * (TILE // BC)
    me = lax.axis_index("grp")
    counts, lists = work_lists(tile_of, cell_of, me, out_dev, cells)
    swap = jnp.where(me == 0, jnp.arange(2), jnp.arange(2)[::-1])
    counts, lists = jnp.take(counts, swap, axis=0), jnp.take(lists, swap, axis=0)

    volts = voltages.reshape(inputs, 2, FRADIX, FRADIX).transpose(0, 2, 1, 3)
    volts = volts.reshape(inputs, 2 * FRADIX, FRADIX)
    factor = 1.0 / math.sqrt(spectra * AVG)
    tables = spectra_tables(n_gx, out_dev)
    front, middle, last = 0, out_dev // 2, out_dev - 1

    def exchange(spec):
        return lax.all_to_all(spec, "gx", split_axis=0, concat_axis=0, tiled=True)

    def swap_groups(data):
        return lax.ppermute(data, "grp", [(0, 1), (1, 0)])

    def work(grid, *items):
        number = jnp.concatenate([counts[g, start:stop] for g, start, stop, _ in items])
        list_of = jnp.concatenate([lists[g, start:stop] for g, start, stop, _ in items])
        streams = [data for _, _, _, data in items]
        return gram_call(number, list_of, streams, grid, cells, factor)

    high, low, spec_a = spectra_call(volts, None, tables, n_gx, out_dev, front, middle)
    turned = (high, low)
    mine_a = exchange(spec_a)
    spec_c = spectra_call(None, turned, tables, n_gx, out_dev, last, out_dev)
    other_c = swap_groups(spec_c)
    spec_b = spectra_call(None, turned, tables, n_gx, out_dev, middle, last)
    other_a = swap_groups(mine_a)
    mine_b = exchange(spec_b)
    grid = work(None, (0, front, middle, mine_a))
    other_b = swap_groups(mine_b)
    both_c = exchange(jnp.concatenate([spec_c, other_c], axis=1))
    grid = work(grid, (0, middle, last, mine_b), (1, front, middle, other_a))
    grid = work(grid, (1, middle, last, other_b))
    twist, second = row_tables()
    rows = rows_call(counts[:, last], lists[:, last], both_c, grid, cells, factor, twist, second, n_gx)
    data = exchange(rows)
    cos, sin = column_twist()
    image = column_call(data, column_tables(n_gx), cos, sin)
    return image.reshape(1, 2, TILE // n_gx, TILE)


def base_table(radix, sign):
    index = jnp.arange(radix, dtype=jnp.int32)
    product = index[:, None] * index[None, :] % radix
    angle = sign * 2.0 * math.pi / radix * product.astype(jnp.float32)
    return (jnp.cos(angle), jnp.sin(angle))


def twist_table(radix, sign):
    index = jnp.arange(radix, dtype=jnp.int32)
    product = index[:, None] * index[None, :]
    angle = sign * 2.0 * math.pi / (radix * radix) * product.astype(jnp.float32)
    return (jnp.cos(angle), jnp.sin(angle))


def complex_einsum(form, table, real_part, imag_part):
    cos_part, sin_part = table

    def product(left, right):
        return jnp.einsum(form, left, right, precision=lax.Precision.HIGH)

    new_real = product(cos_part, real_part) - product(sin_part, imag_part)
    new_imag = product(cos_part, imag_part) + product(sin_part, real_part)
    return (new_real, new_imag)


def fourier(real_part, imag_part, radix, sign, to_front):
    count = real_part.shape[0]
    real_part = real_part.reshape(count, radix, radix)
    imag_part = imag_part.reshape(count, radix, radix)
    table = base_table(radix, sign)
    real_part, imag_part = complex_einsum("ak,rab->rkb", table, real_part, imag_part)
    twist_cos, twist_sin = twist_table(radix, sign)
    twist_cos = twist_cos.T
    twist_sin = twist_sin.T
    turned_real = real_part * twist_cos - imag_part * twist_sin
    turned_imag = real_part * twist_sin + imag_part * twist_cos
    if to_front:
        form = "bj,rkb->jkr"
        shape = (radix * radix, count)
    else:
        form = "bj,rkb->rjk"
        shape = (count, radix * radix)
    out_real, out_imag = complex_einsum(form, table, turned_real, turned_imag)
    return (out_real.reshape(shape) / radix, out_imag.reshape(shape) / radix)


def operands(local):
    stations, pols, spectra, _, channels = local.shape
    inputs = stations * pols
    nout = channels // AVG
    grouped = local.reshape(inputs, spectra, 2, nout, AVG).transpose(3, 0, 1, 2, 4)
    swapped = jnp.stack([grouped[:, :, :, 1], -grouped[:, :, :, 0]], axis=3)
    left = jnp.stack([grouped, swapped], axis=1).reshape(nout, 2 * inputs, spectra, 2 * AVG)
    right = grouped.reshape(nout, inputs, spectra, 2 * AVG)
    return (left, right)


def gram_all(local):
    left, right = operands(local)
    nout, rows_two, spectra, depth = left.shape
    left = left.reshape(nout, rows_two, spectra * depth)
    right = right.reshape(nout, rows_two // 2, spectra * depth)
    return jnp.einsum("oyk,ork->oyr", left, right, preferred_element_type=jnp.float32)


def pair_fits(gx_count, shape):
    lead, st_dev, pols, spectra, _, fine = shape
    return (
        lead == 1
        and spectra == 1
        and fine == FRADIX * FRADIX
        and (st_dev * pols) % PACK == 0
        and fine % (gx_count * AVG) == 0
        and TILE // gx_count // BR == PACK
        and fine // (gx_count * AVG) >= 4
        and gx_count % 4 == 0
    )


def on_device(voltages, tile_of, cell_of):
    grp_count = lax.axis_size("grp")
    gx_count = lax.axis_size("gx")
    _, st_dev, pols, spectra, _, fine = voltages.shape
    if grp_count == 2 and pair_fits(gx_count, voltages.shape):
        return pair_plan(voltages, tile_of, cell_of)
    volts = voltages.reshape(st_dev * pols * spectra, 2, fine).astype(jnp.float32)
    spec_re, spec_im = fourier(volts[:, 0], volts[:, 1], FRADIX, -1.0, False)
    spec = jnp.stack([spec_re, spec_im], axis=1).astype(jnp.bfloat16)
    spec = spec.reshape(st_dev, pols, spectra, 2, fine)
    local = lax.all_to_all(spec, "gx", split_axis=4, concat_axis=0, tiled=True)
    gram = gram_all(local)
    factor = 1.0 / math.sqrt(spectra * AVG)
    out_dev = gram.shape[0]
    inputs = gram.shape[2]
    vis = (gram * factor).astype(jnp.bfloat16).reshape(out_dev, 2, inputs, inputs)
    width = 2 * BR * BC
    shaped = vis.reshape(out_dev, 2, inputs // BR, BR, inputs // BC, BC)
    blocks = shaped.transpose(0, 2, 4, 1, 3, 5).reshape(-1, width)
    count_blocks = blocks.shape[0]
    capacity = max(2, count_blocks // (4 * grp_count))
    slots = grp_count * capacity
    me = lax.axis_index("grp")
    groups = tile_of.shape[0]
    marked = (tile_of[:, None, :] == jnp.arange(grp_count, dtype=jnp.int32)[None, :, None]).astype(
        jnp.int32
    )
    rank_all = jnp.sum((jnp.cumsum(marked, axis=2) - marked) * marked, axis=1)
    my_tiles = lax.dynamic_index_in_dim(tile_of, me, 0, keepdims=False)
    my_rank = lax.dynamic_index_in_dim(rank_all, me, 0, keepdims=False)
    slot_id = jnp.where(my_tiles < 0, -1, my_tiles * capacity + my_rank)
    hits = jnp.arange(slots, dtype=jnp.int32)[:, None] == slot_id[None, :]
    filled = jnp.any(hits, axis=1)
    source = jnp.where(filled, jnp.argmax(hits, axis=1), count_blocks)
    padded = jnp.concatenate([blocks, jnp.zeros((1, width), jnp.bfloat16)], axis=0)
    outgoing = jnp.take(padded, source, axis=0)
    outgoing = outgoing.reshape(grp_count, capacity, width)
    arrived = lax.all_to_all(outgoing, "grp", split_axis=0, concat_axis=0, tiled=True)
    slab = TILE // gx_count
    row_blocks = slab // BR
    col_blocks = TILE // BC
    cells_count = row_blocks * col_blocks
    source_group = jnp.arange(groups, dtype=jnp.int32)[:, None]
    slot_flat = jnp.where(tile_of == me, source_group * capacity + rank_all, -1).reshape(-1)
    cell_flat = cell_of.reshape(-1)
    cell_hit = (jnp.arange(cells_count, dtype=jnp.int32)[:, None] == cell_flat[None, :]).astype(
        jnp.bfloat16
    )
    slot_hit = (jnp.arange(slots, dtype=jnp.int32)[:, None] == slot_flat[None, :]).astype(
        jnp.bfloat16
    )
    place = lax.dot_general(
        cell_hit, slot_hit, (((1,), (1,)), ((), ())), preferred_element_type=jnp.float32
    )
    place = place.astype(jnp.bfloat16)
    grid = jnp.dot(place, arrived.reshape(slots, width), preferred_element_type=jnp.float32)
    grid = (
        grid.reshape(row_blocks, col_blocks, 2, BR, BC)
        .transpose(2, 0, 3, 1, 4)
        .reshape(2, slab, TILE)
    )
    rows_re, rows_im = fourier(grid[0], grid[1], TRADIX, 1.0, True)
    rows = jnp.stack([rows_re, rows_im], axis=0).astype(jnp.bfloat16)
    columns = lax.all_to_all(rows, "gx", split_axis=1, concat_axis=2, tiled=True)
    kx_local = columns.shape[1]
    image_re, image_im = fourier(
        columns[0].astype(jnp.float32), columns[1].astype(jnp.float32), TRADIX, 1.0, False
    )
    image = jnp.stack([image_re, image_im], axis=0).reshape(1, 2, kx_local, TILE)
    return image


def solution(mesh):
    in_specs = (P("grp", "gx", None, None, None, None), P(None, "gx"), P(None, "gx"))
    out_specs = P("grp", None, "gx", None)
    return jax.shard_map(
        on_device, mesh=mesh, in_specs=in_specs, out_specs=out_specs, check_vma=False
    )
```

```python
import functools
import math

import jax
import jax.numpy as jnp
import numpy as np
from jax import lax
from jax.experimental import pallas as pl
from jax.experimental.pallas import tpu as pltpu
from jax.sharding import PartitionSpec as P


FRADIX = 128
AVG = 256
BR = 16
BC = 128
TRADIX = 64
TILE = 4096
SUB = 8
PACK = 16
F32 = jnp.float32
BF16 = jnp.bfloat16


def halves(matrix):
    high = matrix.astype(np.float32).astype(BF16)
    low = (matrix - high.astype(np.float64)).astype(np.float32).astype(BF16)
    return high, low


def complex_table(angle, scale):
    cos, sin = scale * np.cos(angle), scale * np.sin(angle)
    return np.stack([np.stack([cos, -sin]), np.stack([sin, cos])])


def turn(product, period, sign):
    return sign * 2.0 * np.pi / period * (product % period)


def spectra_tables(n_gx, out_dev):
    index = np.arange(FRADIX)
    first = complex_table(turn(np.outer(index, index), FRADIX, -1.0), 1.0 / FRADIX)
    first = first.transpose(0, 2, 3, 1).reshape(2 * FRADIX, 2 * FRADIX)
    high, low = halves(first)
    first = np.concatenate([high, low], axis=1)
    angle = turn(np.outer(index, index), FRADIX * FRADIX, -1.0)
    twist = np.stack([np.cos(angle), np.sin(angle)]).astype(np.float32)
    second = complex_table(turn(np.outer(index, index), FRADIX, -1.0), 1.0)
    low_count = FRADIX // (n_gx * out_dev)
    second = second.reshape(2, 2, n_gx, out_dev, low_count, FRADIX)
    second = second.transpose(3, 2, 0, 4, 1, 5).reshape(2 * FRADIX, 2 * FRADIX)
    high, low = halves(second)
    second = np.concatenate([high, low, high], axis=1)
    return first, twist, second


def row_tables():
    cols = TILE // BC
    k1, w = np.arange(cols), np.arange(BC)
    angle = turn(np.outer(k1, w), TILE, 1.0)
    twist = np.stack([np.cos(angle), np.sin(angle)]).astype(np.float32)
    second = complex_table(turn(np.outer(w, w), BC, 1.0), 1.0 / math.sqrt(TILE))
    second = second.transpose(2, 0, 1, 3).reshape(2 * BC, 2 * BC)
    return twist, halves(second)[0]


def column_tables(n_gx):
    count = TILE // BR
    blocks = count // n_gx
    index = np.arange(count)
    first = complex_table(turn(np.outer(index, index), count, 1.0), 1.0 / math.sqrt(TILE))
    first = first.reshape(2, 2, n_gx, blocks, count)
    first = first.transpose(2, 1, 3, 0, 4).reshape(2 * count, 2 * count)
    return halves(first)[0]


def column_twist():
    shape = (BR, TILE // BR)
    product = lax.broadcasted_iota(jnp.int32, shape, 0) * lax.broadcasted_iota(jnp.int32, shape, 1)
    angle = 2.0 * math.pi / TILE * product.astype(F32)
    return jnp.cos(angle), jnp.sin(angle)


def times(value, factor):
    re, im = value
    c, s = factor
    return (re * c - im * s, re * s + im * c)


def fixed_turn(value, step, count, sign):
    re, im = value
    step = step % count
    if step == 0:
        return value
    if 4 * step == count:
        return (-im, re) if sign > 0 else (im, -re)
    angle = sign * 2.0 * math.pi * step / count
    c, s = math.cos(angle), math.sin(angle)
    if 8 * step == count:
        return ((re - im) * c, (re + im) * c) if sign > 0 else ((re + im) * c, (im - re) * c)
    if 8 * step == 3 * count:
        h = abs(c)
        return ((-re - im) * h, (re - im) * h) if sign > 0 else ((im - re) * h, (-re - im) * h)
    return (re * c - im * s, re * s + im * c)


def butterflies(values, sign):
    count = len(values)
    if count == 1:
        return values
    even = butterflies(values[0::2], sign)
    odd = butterflies(values[1::2], sign)
    out = [None] * count
    for k in range(count // 2):
        turned = fixed_turn(odd[k], k, count, sign)
        out[k] = (even[k][0] + turned[0], even[k][1] + turned[1])
        out[k + count // 2] = (even[k][0] - turned[0], even[k][1] - turned[1])
    return out


def split_value(value):
    high = value.astype(BF16)
    return high, (value - high.astype(F32)).astype(BF16)


def dot_nt(left, right):
    return lax.dot_general(left, right, (((1,), (1,)), ((), ())), preferred_element_type=F32)


def dot_tn(left, right):
    return lax.dot_general(left, right, (((0,), (0,)), ((), ())), preferred_element_type=F32)


def channel_rows(n_gx, scratch, out_ref):
    stride = scratch.shape[0] // PACK
    channels = out_ref.shape[1]
    per = out_ref.shape[3] // FRADIX
    for o in range(channels):
        for d in range(n_gx):
            for t in range(per):
                piece = scratch[pl.ds((o * n_gx + d) * per + t, PACK, stride=stride), :]
                out_ref[d, o, :, t * FRADIX : (t + 1) * FRADIX] = piece.astype(BF16)


PIECES = 4
LEAD = 4


def spectra_kernel(n_gx, *refs):
    v_refs, (first_ref, twist_ref, second_ref, out_ref, high, low, scratch) = refs[:PIECES], refs[PIECES:]
    rows = second_ref.shape[0]
    stride = scratch.shape[0] // PACK
    two = 2 * FRADIX
    share = PACK // PIECES

    def turn_pair(pair):
        v_ref, at = v_refs[2 * pair // share], 2 * pair % share
        v = jnp.concatenate([v_ref[at], v_ref[at + 1]], axis=1)
        y = jnp.dot(first_ref[...], jnp.concatenate([v, v], axis=0), preferred_element_type=F32)
        for u in range(2):
            lane = slice(u * FRADIX, (u + 1) * FRADIX)
            value = times((y[:FRADIX, lane], y[FRADIX:, lane]), (twist_ref[0], twist_ref[1]))
            at_rows = slice((2 * pair + u) * FRADIX, (2 * pair + u + 1) * FRADIX)
            for part in range(2):
                at_lane = slice(part * FRADIX, (part + 1) * FRADIX)
                high[at_rows, at_lane], low[at_rows, at_lane] = split_value(value[part])

    for pair in range(LEAD):
        turn_pair(pair)
    for pair in range(PACK // 2):
        if pair + LEAD < PACK // 2:
            turn_pair(pair + LEAD)
        at_rows = slice(pair * two, (pair + 1) * two)
        h, l = high[at_rows], low[at_rows]
        z = dot_nt(second_ref[...], jnp.concatenate([h, h, l], axis=1))
        for u in range(2):
            at = (2 * pair + u) * stride
            scratch[at : at + rows, :] = z[:, u * FRADIX : (u + 1) * FRADIX]
    channel_rows(n_gx, scratch, out_ref)


def whole(x):
    return pl.BlockSpec(x.shape, lambda *i: (0,) * x.ndim)


def spectra_call(volts, tables, n_gx, out_dev, start, stop):
    first, twist, second = tables
    per = 2 * FRADIX // out_dev
    second = second[start * per : stop * per]
    depth = 2 * AVG
    channels = stop - start
    inputs = volts.shape[0]
    return pl.pallas_call(
        functools.partial(spectra_kernel, n_gx),
        grid=(inputs // PACK,),
        in_specs=[
            pl.BlockSpec((PACK // PIECES, 2 * FRADIX, FRADIX), lambda i, p=p: (i * PIECES + p, 0, 0))
            for p in range(PIECES)
        ]
        + [whole(first), whole(twist), whole(second)],
        out_specs=pl.BlockSpec((n_gx, channels, PACK, depth), lambda i: (0, 0, i, 0)),
        out_shape=jax.ShapeDtypeStruct((n_gx, channels, inputs, depth), BF16),
        scratch_shapes=[
            pltpu.VMEM((PACK * FRADIX, 2 * FRADIX), BF16),
            pltpu.VMEM((PACK * FRADIX, 2 * FRADIX), BF16),
            pltpu.VMEM((PACK * (channels * per + SUB), FRADIX), F32),
        ],
        name="spectra",
    )(*[volts] * PIECES, first, twist, second)


def correlate(x_ref, slot, vis, factor, unroll):
    sources, _, inputs, depth = x_ref.shape
    nin = sources * inputs
    half = depth // 2
    group = sources // 4
    panel = group * inputs

    def one(p, carry):
        base = pl.multiple_of(p * panel, panel)
        x = x_ref[pl.ds(p * group, group), slot].reshape(panel, depth)
        swapped = jnp.concatenate([x[:, half:], -x[:, :half]], axis=1)
        left = jnp.concatenate([x, swapped], axis=0)
        right = x_ref[:, slot].reshape(nin, depth)
        gram = (dot_nt(left, right) * factor).astype(BF16)
        for e in range(nin // BC):
            vis[0, e, pl.ds(base, panel), :] = gram[:panel, e * BC : (e + 1) * BC]
            vis[1, e, pl.ds(base, panel), :] = gram[panel:, e * BC : (e + 1) * BC]
        return carry

    lax.fori_loop(0, sources // group, one, 0, unroll=unroll)


def place_blocks(which, count_ref, list_ref, vis, grid):
    cells = grid.shape[1]
    wide = vis.shape[1]

    def place(s, carry):
        code = list_ref[which, s]
        cell = lax.rem(code, cells)
        block = lax.div(code, cells)
        e = lax.rem(block, wide)
        row = pl.multiple_of(lax.div(block, wide) * BR, BR)
        for part in range(2):
            grid[part, cell] += vis[part, e, pl.ds(row, BR), :].astype(F32)
        return carry

    lax.fori_loop(0, count_ref[which], place, 0)


LOADS = 8


def split_copies(source, target, sems):
    share = target.shape[1] // LOADS
    copies = []
    for i in range(LOADS):
        at = pl.ds(i * share, share)
        copies.append(pltpu.make_async_copy(source.at[:, at], target.at[:, at], sems.at[i]))
    return copies


def gram_kernel(slots, first_call, factor, count_ref, list_ref, *rest):
    x_refs, rest = rest[: len(slots)], rest[len(slots) :]
    out_ref, vis, grid, sems = rest[-4:]
    cells = grid.shape[1]
    if first_call:

        def clear(i, carry):
            grid[:, pl.ds(i * SUB, SUB)] = jnp.zeros((2, SUB, BR, BC), F32)
            return carry

        lax.fori_loop(0, cells // SUB, clear, 0)
    else:
        loads = split_copies(rest[0], grid, sems)
        for load in loads:
            load.start()
    which = 0
    for x_ref, many in zip(x_refs, slots):
        for slot in range(many):
            correlate(x_ref, slot, vis, factor, False)
            if which == 0 and not first_call:
                for load in loads:
                    load.wait()
            place_blocks(which, count_ref, list_ref, vis, grid)
            which += 1
    stores = split_copies(grid, out_ref, sems)
    for store in stores:
        store.start()
    for store in stores:
        store.wait()


def gram_call(counts, lists, streams, grid, cells, factor):
    first_call = grid is None
    shape = (2, cells, BR, BC)
    sources, _, inputs, depth = streams[0].shape
    nin = sources * inputs
    slots = tuple(x.shape[1] for x in streams)
    any_spec = pl.BlockSpec(memory_space=pl.ANY)
    vmem = pl.BlockSpec(memory_space=pltpu.VMEM)
    smem = pl.BlockSpec(memory_space=pltpu.SMEM)
    args = (counts, lists) + tuple(streams) + (() if first_call else (grid,))
    flops = sum(slots) * 4 * nin * nin * depth
    return pl.pallas_call(
        functools.partial(gram_kernel, slots, first_call, factor),
        in_specs=[smem, smem] + [vmem] * len(streams) + ([] if first_call else [any_spec]),
        out_specs=any_spec,
        out_shape=jax.ShapeDtypeStruct(shape, F32),
        scratch_shapes=[
            pltpu.VMEM((2, nin // BC, nin, BC), BF16),
            pltpu.VMEM(shape, F32),
            pltpu.SemaphoreType.DMA((LOADS,)),
        ],
        input_output_aliases={} if first_call else {2 + len(streams): 0},
        cost_estimate=pl.CostEstimate(flops=flops, transcendentals=0, bytes_accessed=2**24),
        name="gram",
    )(*args)


def row_block(block, grid, twist_ref, stage, turned):
    cols = TILE // BC
    inner = cols // 4
    for h in range(BR // SUB):
        rows = slice(h * SUB, (h + 1) * SUB)
        for q in range(4):
            at = [block * cols + 4 * m + q for m in range(inner)]
            values = butterflies([(grid[0, c, rows], grid[1, c, rows]) for c in at], 1.0)
            for k in range(inner):
                re, im = fixed_turn(values[k], q * k, cols, 1.0)
                stage[h, 0, q * inner + k] = re
                stage[h, 1, q * inner + k] = im
    for k in range(inner):
        halves_of = []
        for h in range(BR // SUB):
            values = [(stage[h, 0, q * inner + k], stage[h, 1, q * inner + k]) for q in range(4)]
            values = butterflies(values, 1.0)
            for m in range(4):
                at = k + m * inner
                if at:
                    factor = (twist_ref[0, at : at + 1, :], twist_ref[1, at : at + 1, :])
                    values[m] = times(values[m], factor)
            halves_of.append(values)
        for m in range(4):
            at = slice((k + m * inner) * BR, (k + m * inner + 1) * BR)
            for part in range(2):
                both = jnp.concatenate([values[m][part] for values in halves_of], axis=0)
                turned[block, at, part * BC : (part + 1) * BC] = both.astype(BF16)


SENDS = 4


def rows_kernel(
    factor,
    count_ref,
    list_ref,
    x_ref,
    grid_ref,
    twist_ref,
    second_ref,
    out_ref,
    vis,
    grid,
    stage,
    turned,
    scratch,
    ready,
    sems,
    out_sems,
):
    blocks = turned.shape[0]
    lanes = SUB * BR
    rows = 2 * BC
    step = pl.program_id(0)

    @pl.when(step == 0)
    def _():
        loads = split_copies(grid_ref, grid, sems)
        for load in loads:
            load.start()
        for slot in range(x_ref.shape[1]):
            correlate(x_ref, slot, vis, factor, True)
            if slot == 0:
                for load in loads:
                    load.wait()
            place_blocks(slot, count_ref, list_ref, vis, grid)

        def one(block, carry):
            row_block(block, grid, twist_ref, stage, turned)
            return carry

        lax.fori_loop(0, blocks, one, 0)

    stride = scratch.shape[0] // blocks
    at_lane = pl.ds(pl.multiple_of(step * lanes, lanes), lanes)
    for b in range(blocks // 2):
        data = turned[2 * b : 2 * b + 2, at_lane].reshape(2 * lanes, rows)
        z = dot_nt(second_ref[...], data)
        for u in range(2):
            at = (2 * b + u) * stride
            scratch[at : at + rows, :] = z[:, u * lanes : (u + 1) * lanes]
    n_gx, lows, _, _ = out_ref.shape
    share = n_gx // SENDS

    def sends(at_step):
        slot = lax.rem(at_step, 2)
        at_out = pl.ds(pl.multiple_of(at_step * lanes, lanes), lanes)
        copies = []
        for i in range(SENDS):
            at = pl.ds(i * share, share)
            copies.append(pltpu.make_async_copy(ready.at[slot, at], out_ref.at[at, :, :, at_out], out_sems.at[slot, i]))
        return copies

    steps = pl.num_programs(0)
    slot = lax.rem(step, 2)

    @pl.when(step >= 2)
    def _():
        for copy in sends(step - 2):
            copy.wait()

    mine = sends(step)
    for d in range(n_gx):
        for k in range(lows):
            for part in range(2):
                row = (d * lows + k) * 2 + part
                piece = scratch[pl.ds(row, blocks, stride=stride), :]
                ready[slot, d, k, part * blocks : (part + 1) * blocks, :] = piece.astype(BF16)
        if d % share == share - 1:
            mine[d // share].start()

    @pl.when(step == steps - 1)
    def _():
        for at_step in (steps - 2, steps - 1):
            for copy in sends(at_step):
                copy.wait()


def rows_call(counts, lists, stream, grid, cells, factor, twist, second, n_gx):
    sources, _, inputs, _ = stream.shape
    nin = sources * inputs
    cols = TILE // BC
    blocks = cells // cols
    lanes = SUB * BR
    lows = BC // n_gx
    smem = pl.BlockSpec(memory_space=pltpu.SMEM)
    return pl.pallas_call(
        functools.partial(rows_kernel, factor),
        grid=(cols // SUB,),
        in_specs=[
            smem,
            smem,
            pl.BlockSpec(memory_space=pltpu.VMEM),
            pl.BlockSpec(memory_space=pltpu.HBM),
            whole(twist),
            whole(second),
        ],
        out_specs=pl.BlockSpec(memory_space=pltpu.HBM),
        out_shape=jax.ShapeDtypeStruct((n_gx, lows, 2 * blocks, cols * BR), BF16),
        scratch_shapes=[
            pltpu.VMEM((2, nin // BC, nin, BC), BF16),
            pltpu.VMEM((2, cells, BR, BC), F32),
            pltpu.VMEM((BR // SUB, 2, cols, SUB, BC), F32),
            pltpu.VMEM((blocks, cols * BR, 2 * BC), BF16),
            pltpu.VMEM((blocks * (2 * BC + SUB), lanes), F32),
            pltpu.VMEM((2, n_gx, lows, 2 * blocks, lanes), BF16),
            pltpu.SemaphoreType.DMA((LOADS,)),
            pltpu.SemaphoreType.DMA((2, SENDS)),
        ],
        compiler_params=pltpu.CompilerParams(vmem_limit_bytes=48 * 2**20),
        name="rows",
    )(counts, lists, stream, grid, twist, second)


def column_kernel(data_ref, first_ref, cos_ref, sin_ref, out_ref, scratch, ready, out_sems):
    n_gx, _, rows, lanes = data_ref.shape
    count = TILE // BR
    span = SUB * BR

    def mix(g):
        data = data_ref[:, 0, :, g * span : (g + 1) * span].reshape(n_gx * rows, span)
        mixed = dot_tn(data, first_ref[...])
        for b in range(2 * count // BC):
            scratch[g, b * span : (b + 1) * span, :] = mixed[:, b * BC : (b + 1) * BC]

    step = pl.program_id(0)
    steps = pl.num_programs(0)
    slot = lax.rem(step, 2)
    groups = lanes // (SUB * BR)

    def sends(at_step):
        at_slot = lax.rem(at_step, 2)
        copies = []
        for g in range(groups):
            at = pl.ds(g * SUB, SUB)
            for part in range(2):
                source, target = ready.at[at_slot, part, at], out_ref.at[part, at_step, at]
                copies.append(pltpu.make_async_copy(source, target, out_sems.at[at_slot, 2 * g + part]))
        return copies

    @pl.when(step >= 2)
    def _():
        for copy in sends(step - 2):
            copy.wait()

    mine = sends(step)
    mix(0)
    for g in range(groups):
        if g + 1 < groups:
            mix(g + 1)
        for b in range(count // BC):
            lane = slice(b * BC, (b + 1) * BC)
            values = []
            for r in range(BR):
                value = (
                    scratch[g, pl.ds(b * span + r, SUB, stride=BR), :],
                    scratch[g, pl.ds((count // BC + b) * span + r, SUB, stride=BR), :],
                )
                factor = (cos_ref[r : r + 1, lane], sin_ref[r : r + 1, lane])
                values.append(times(value, factor) if r else value)
            values = butterflies(values, 1.0)
            for k in range(BR):
                at = slice(k * count + b * BC, k * count + (b + 1) * BC)
                for part in range(2):
                    ready[slot, part, g * SUB : (g + 1) * SUB, at] = values[k][part]
        mine[2 * g].start()
        mine[2 * g + 1].start()

    @pl.when(step == steps - 1)
    def _():
        for at_step in (steps - 2, steps - 1):
            for copy in sends(at_step):
                copy.wait()


def column_call(data, first, cos, sin):
    n_gx, lows, rows, lanes = data.shape
    cols = TILE // BC
    return pl.pallas_call(
        column_kernel,
        grid=(lows,),
        in_specs=[
            pl.BlockSpec((n_gx, 1, rows, lanes), lambda i: (0, i, 0, 0)),
            whole(first),
            whole(cos),
            whole(sin),
        ],
        out_specs=pl.BlockSpec(memory_space=pl.ANY),
        out_shape=jax.ShapeDtypeStruct((2, lows, cols, TILE), F32),
        scratch_shapes=[
            pltpu.VMEM((cols // SUB, 2 * (TILE // BR) // BC * SUB * BR, BC), F32),
            pltpu.VMEM((2, 2, cols, TILE), F32),
            pltpu.SemaphoreType.DMA((2, 2 * cols // SUB)),
        ],
        name="column",
    )(data, first, cos, sin)


def work_lists(tile_of, cell_of, me, out_dev, cells):
    groups, blocks = tile_of.shape
    per = blocks // out_dev
    taken = (tile_of == me).reshape(groups, out_dev, per)
    number = taken.astype(jnp.int32)
    rank = jnp.cumsum(number, axis=2) - number
    slot = jnp.where(taken, rank, -1)
    code = jnp.arange(per, dtype=jnp.int32) * cells + cell_of.reshape(groups, out_dev, per)
    hit = jnp.arange(per, dtype=jnp.int32)[:, None] == slot[:, :, None, :]
    lists = jnp.sum(jnp.where(hit, code[:, :, None, :], 0), axis=3)
    return jnp.sum(number, axis=2), lists


def pair_plan(voltages, tile_of, cell_of):
    n_gx = lax.axis_size("gx")
    _, st_dev, pols, spectra, _, fine = voltages.shape
    inputs = st_dev * pols
    out_dev = fine // (n_gx * AVG)
    cells = (TILE // n_gx // BR) * (TILE // BC)
    me = lax.axis_index("grp")
    counts, lists = work_lists(tile_of, cell_of, me, out_dev, cells)
    swap = jnp.where(me == 0, jnp.arange(2), jnp.arange(2)[::-1])
    counts, lists = jnp.take(counts, swap, axis=0), jnp.take(lists, swap, axis=0)

    volts = voltages.reshape(inputs, 2, FRADIX, FRADIX).transpose(0, 2, 1, 3)
    volts = volts.reshape(inputs, 2 * FRADIX, FRADIX)
    factor = 1.0 / math.sqrt(spectra * AVG)
    tables = spectra_tables(n_gx, out_dev)
    front, middle, last = 0, out_dev // 2, out_dev - 1

    def exchange(spec):
        return lax.all_to_all(spec, "gx", split_axis=0, concat_axis=0, tiled=True)

    def swap_groups(data):
        return lax.ppermute(data, "grp", [(0, 1), (1, 0)])

    def work(grid, *items):
        number = jnp.concatenate([counts[g, start:stop] for g, start, stop, _ in items])
        list_of = jnp.concatenate([lists[g, start:stop] for g, start, stop, _ in items])
        streams = [data for _, _, _, data in items]
        return gram_call(number, list_of, streams, grid, cells, factor)

    spec_a = spectra_call(volts, tables, n_gx, out_dev, front, middle)
    mine_a = exchange(spec_a)
    spec_c = spectra_call(volts, tables, n_gx, out_dev, last, out_dev)
    other_c = swap_groups(spec_c)
    spec_b = spectra_call(volts, tables, n_gx, out_dev, middle, last)
    other_a = swap_groups(mine_a)
    mine_b = exchange(spec_b)
    grid = work(None, (0, front, middle, mine_a))
    other_b = swap_groups(mine_b)
    both_c = exchange(jnp.concatenate([spec_c, other_c], axis=1))
    grid = work(grid, (0, middle, last, mine_b), (1, front, middle, other_a))
    grid = work(grid, (1, middle, last, other_b))
    twist, second = row_tables()
    rows = rows_call(counts[:, last], lists[:, last], both_c, grid, cells, factor, twist, second, n_gx)
    data = exchange(rows)
    cos, sin = column_twist()
    image = column_call(data, column_tables(n_gx), cos, sin)
    return image.reshape(1, 2, TILE // n_gx, TILE)


def base_table(radix, sign):
    index = jnp.arange(radix, dtype=jnp.int32)
    product = index[:, None] * index[None, :] % radix
    angle = sign * 2.0 * math.pi / radix * product.astype(jnp.float32)
    return (jnp.cos(angle), jnp.sin(angle))


def twist_table(radix, sign):
    index = jnp.arange(radix, dtype=jnp.int32)
    product = index[:, None] * index[None, :]
    angle = sign * 2.0 * math.pi / (radix * radix) * product.astype(jnp.float32)
    return (jnp.cos(angle), jnp.sin(angle))


def complex_einsum(form, table, real_part, imag_part):
    cos_part, sin_part = table

    def product(left, right):
        return jnp.einsum(form, left, right, precision=lax.Precision.HIGH)

    new_real = product(cos_part, real_part) - product(sin_part, imag_part)
    new_imag = product(cos_part, imag_part) + product(sin_part, real_part)
    return (new_real, new_imag)


def fourier(real_part, imag_part, radix, sign, to_front):
    count = real_part.shape[0]
    real_part = real_part.reshape(count, radix, radix)
    imag_part = imag_part.reshape(count, radix, radix)
    table = base_table(radix, sign)
    real_part, imag_part = complex_einsum("ak,rab->rkb", table, real_part, imag_part)
    twist_cos, twist_sin = twist_table(radix, sign)
    twist_cos = twist_cos.T
    twist_sin = twist_sin.T
    turned_real = real_part * twist_cos - imag_part * twist_sin
    turned_imag = real_part * twist_sin + imag_part * twist_cos
    if to_front:
        form = "bj,rkb->jkr"
        shape = (radix * radix, count)
    else:
        form = "bj,rkb->rjk"
        shape = (count, radix * radix)
    out_real, out_imag = complex_einsum(form, table, turned_real, turned_imag)
    return (out_real.reshape(shape) / radix, out_imag.reshape(shape) / radix)


def operands(local):
    stations, pols, spectra, _, channels = local.shape
    inputs = stations * pols
    nout = channels // AVG
    grouped = local.reshape(inputs, spectra, 2, nout, AVG).transpose(3, 0, 1, 2, 4)
    swapped = jnp.stack([grouped[:, :, :, 1], -grouped[:, :, :, 0]], axis=3)
    left = jnp.stack([grouped, swapped], axis=1).reshape(nout, 2 * inputs, spectra, 2 * AVG)
    right = grouped.reshape(nout, inputs, spectra, 2 * AVG)
    return (left, right)


def gram_all(local):
    left, right = operands(local)
    nout, rows_two, spectra, depth = left.shape
    left = left.reshape(nout, rows_two, spectra * depth)
    right = right.reshape(nout, rows_two // 2, spectra * depth)
    return jnp.einsum("oyk,ork->oyr", left, right, preferred_element_type=jnp.float32)


def pair_fits(gx_count, shape):
    lead, st_dev, pols, spectra, _, fine = shape
    return (
        lead == 1
        and spectra == 1
        and fine == FRADIX * FRADIX
        and (st_dev * pols) % PACK == 0
        and fine % (gx_count * AVG) == 0
        and TILE // gx_count // BR == PACK
        and fine // (gx_count * AVG) >= 4
        and gx_count % 4 == 0
    )


def on_device(voltages, tile_of, cell_of):
    grp_count = lax.axis_size("grp")
    gx_count = lax.axis_size("gx")
    _, st_dev, pols, spectra, _, fine = voltages.shape
    if grp_count == 2 and pair_fits(gx_count, voltages.shape):
        return pair_plan(voltages, tile_of, cell_of)
    volts = voltages.reshape(st_dev * pols * spectra, 2, fine).astype(jnp.float32)
    spec_re, spec_im = fourier(volts[:, 0], volts[:, 1], FRADIX, -1.0, False)
    spec = jnp.stack([spec_re, spec_im], axis=1).astype(jnp.bfloat16)
    spec = spec.reshape(st_dev, pols, spectra, 2, fine)
    local = lax.all_to_all(spec, "gx", split_axis=4, concat_axis=0, tiled=True)
    gram = gram_all(local)
    factor = 1.0 / math.sqrt(spectra * AVG)
    out_dev = gram.shape[0]
    inputs = gram.shape[2]
    vis = (gram * factor).astype(jnp.bfloat16).reshape(out_dev, 2, inputs, inputs)
    width = 2 * BR * BC
    shaped = vis.reshape(out_dev, 2, inputs // BR, BR, inputs // BC, BC)
    blocks = shaped.transpose(0, 2, 4, 1, 3, 5).reshape(-1, width)
    count_blocks = blocks.shape[0]
    capacity = max(2, count_blocks // (4 * grp_count))
    slots = grp_count * capacity
    me = lax.axis_index("grp")
    groups = tile_of.shape[0]
    marked = (tile_of[:, None, :] == jnp.arange(grp_count, dtype=jnp.int32)[None, :, None]).astype(
        jnp.int32
    )
    rank_all = jnp.sum((jnp.cumsum(marked, axis=2) - marked) * marked, axis=1)
    my_tiles = lax.dynamic_index_in_dim(tile_of, me, 0, keepdims=False)
    my_rank = lax.dynamic_index_in_dim(rank_all, me, 0, keepdims=False)
    slot_id = jnp.where(my_tiles < 0, -1, my_tiles * capacity + my_rank)
    hits = jnp.arange(slots, dtype=jnp.int32)[:, None] == slot_id[None, :]
    filled = jnp.any(hits, axis=1)
    source = jnp.where(filled, jnp.argmax(hits, axis=1), count_blocks)
    padded = jnp.concatenate([blocks, jnp.zeros((1, width), jnp.bfloat16)], axis=0)
    outgoing = jnp.take(padded, source, axis=0)
    outgoing = outgoing.reshape(grp_count, capacity, width)
    arrived = lax.all_to_all(outgoing, "grp", split_axis=0, concat_axis=0, tiled=True)
    slab = TILE // gx_count
    row_blocks = slab // BR
    col_blocks = TILE // BC
    cells_count = row_blocks * col_blocks
    source_group = jnp.arange(groups, dtype=jnp.int32)[:, None]
    slot_flat = jnp.where(tile_of == me, source_group * capacity + rank_all, -1).reshape(-1)
    cell_flat = cell_of.reshape(-1)
    cell_hit = (jnp.arange(cells_count, dtype=jnp.int32)[:, None] == cell_flat[None, :]).astype(
        jnp.bfloat16
    )
    slot_hit = (jnp.arange(slots, dtype=jnp.int32)[:, None] == slot_flat[None, :]).astype(
        jnp.bfloat16
    )
    place = lax.dot_general(
        cell_hit, slot_hit, (((1,), (1,)), ((), ())), preferred_element_type=jnp.float32
    )
    place = place.astype(jnp.bfloat16)
    grid = jnp.dot(place, arrived.reshape(slots, width), preferred_element_type=jnp.float32)
    grid = (
        grid.reshape(row_blocks, col_blocks, 2, BR, BC)
        .transpose(2, 0, 3, 1, 4)
        .reshape(2, slab, TILE)
    )
    rows_re, rows_im = fourier(grid[0], grid[1], TRADIX, 1.0, True)
    rows = jnp.stack([rows_re, rows_im], axis=0).astype(jnp.bfloat16)
    columns = lax.all_to_all(rows, "gx", split_axis=1, concat_axis=2, tiled=True)
    kx_local = columns.shape[1]
    image_re, image_im = fourier(
        columns[0].astype(jnp.float32), columns[1].astype(jnp.float32), TRADIX, 1.0, False
    )
    image = jnp.stack([image_re, image_im], axis=0).reshape(1, 2, kx_local, TILE)
    return image


def solution(mesh):
    in_specs = (P("grp", "gx", None, None, None, None), P(None, "gx"), P(None, "gx"))
    out_specs = P("grp", None, "gx", None)
    return jax.shard_map(
        on_device, mesh=mesh, in_specs=in_specs, out_specs=out_specs, check_vma=False
    )
```

```python
import functools
import math

import jax
import jax.numpy as jnp
import numpy as np
from jax import lax
from jax.experimental import pallas as pl
from jax.experimental.pallas import tpu as pltpu
from jax.sharding import PartitionSpec as P


FRADIX = 128
AVG = 256
BR = 16
BC = 128
TRADIX = 64
TILE = 4096
SUB = 8
PACK = 16
F32 = jnp.float32
BF16 = jnp.bfloat16


def halves(matrix):
    high = matrix.astype(np.float32).astype(BF16)
    low = (matrix - high.astype(np.float64)).astype(np.float32).astype(BF16)
    return high, low


def complex_table(angle, scale):
    cos, sin = scale * np.cos(angle), scale * np.sin(angle)
    return np.stack([np.stack([cos, -sin]), np.stack([sin, cos])])


def turn(product, period, sign):
    return sign * 2.0 * np.pi / period * (product % period)


def spectra_tables(n_gx, out_dev):
    index = np.arange(FRADIX)
    first = complex_table(turn(np.outer(index, index), FRADIX, -1.0), 1.0 / FRADIX)
    first = first.transpose(0, 2, 3, 1).reshape(2 * FRADIX, 2 * FRADIX)
    high, low = halves(first)
    first = np.concatenate([high, low], axis=1)
    angle = turn(np.outer(index, index), FRADIX * FRADIX, -1.0)
    twist = np.stack([np.cos(angle), np.sin(angle)]).astype(np.float32)
    second = complex_table(turn(np.outer(index, index), FRADIX, -1.0), 1.0)
    low_count = FRADIX // (n_gx * out_dev)
    second = second.reshape(2, 2, n_gx, out_dev, low_count, FRADIX)
    second = second.transpose(3, 2, 0, 4, 1, 5).reshape(2 * FRADIX, 2 * FRADIX)
    high, low = halves(second)
    second = np.concatenate([high, low, high], axis=1)
    return first, twist, second


def row_tables():
    cols = TILE // BC
    k1, w = np.arange(cols), np.arange(BC)
    angle = turn(np.outer(k1, w), TILE, 1.0)
    twist = np.stack([np.cos(angle), np.sin(angle)]).astype(np.float32)
    second = complex_table(turn(np.outer(w, w), BC, 1.0), 1.0 / math.sqrt(TILE))
    second = second.transpose(2, 0, 1, 3).reshape(2 * BC, 2 * BC)
    return twist, halves(second)[0]


def column_tables(n_gx):
    count = TILE // BR
    blocks = count // n_gx
    index = np.arange(count)
    first = complex_table(turn(np.outer(index, index), count, 1.0), 1.0 / math.sqrt(TILE))
    first = first.reshape(2, 2, n_gx, blocks, count)
    first = first.transpose(2, 1, 3, 0, 4).reshape(2 * count, 2 * count)
    return halves(first)[0]


def column_twist():
    shape = (BR, TILE // BR)
    product = lax.broadcasted_iota(jnp.int32, shape, 0) * lax.broadcasted_iota(jnp.int32, shape, 1)
    angle = 2.0 * math.pi / TILE * product.astype(F32)
    return jnp.cos(angle), jnp.sin(angle)


def times(value, factor):
    re, im = value
    c, s = factor
    return (re * c - im * s, re * s + im * c)


def fixed_turn(value, step, count, sign):
    re, im = value
    step = step % count
    if step == 0:
        return value
    if 4 * step == count:
        return (-im, re) if sign > 0 else (im, -re)
    angle = sign * 2.0 * math.pi * step / count
    c, s = math.cos(angle), math.sin(angle)
    if 8 * step == count:
        return ((re - im) * c, (re + im) * c) if sign > 0 else ((re + im) * c, (im - re) * c)
    if 8 * step == 3 * count:
        h = abs(c)
        return ((-re - im) * h, (re - im) * h) if sign > 0 else ((im - re) * h, (-re - im) * h)
    return (re * c - im * s, re * s + im * c)


def butterflies(values, sign):
    count = len(values)
    if count == 1:
        return values
    even = butterflies(values[0::2], sign)
    odd = butterflies(values[1::2], sign)
    out = [None] * count
    for k in range(count // 2):
        turned = fixed_turn(odd[k], k, count, sign)
        out[k] = (even[k][0] + turned[0], even[k][1] + turned[1])
        out[k + count // 2] = (even[k][0] - turned[0], even[k][1] - turned[1])
    return out


def split_value(value):
    high = value.astype(BF16)
    return high, (value - high.astype(F32)).astype(BF16)


def dot_nt(left, right):
    return lax.dot_general(left, right, (((1,), (1,)), ((), ())), preferred_element_type=F32)


def dot_tn(left, right):
    return lax.dot_general(left, right, (((0,), (0,)), ((), ())), preferred_element_type=F32)


def channel_rows(n_gx, scratch, out_ref):
    stride = scratch.shape[0] // (PACK + 1)
    channels = out_ref.shape[1]
    per = out_ref.shape[3] // FRADIX
    for o in range(channels):
        for d in range(n_gx):
            for t in range(per):
                piece = scratch[pl.ds((o * n_gx + d) * per + t, PACK, stride=stride), :]
                out_ref[d, o, :, t * FRADIX : (t + 1) * FRADIX] = piece.astype(BF16)


PIECES = 4
LEAD = 4


def spectra_kernel(n_gx, *refs):
    v_refs, (first_ref, twist_ref, second_ref, out_ref, high, low, scratch) = refs[:PIECES], refs[PIECES:]
    rows = second_ref.shape[0]
    stride = scratch.shape[0] // (PACK + 1)
    two = 2 * FRADIX
    share = PACK // PIECES

    def turn_pair(pair):
        v_ref, at = v_refs[2 * pair // share], 2 * pair % share
        v = jnp.concatenate([v_ref[at], v_ref[at + 1]], axis=1)
        y = jnp.dot(first_ref[...], jnp.concatenate([v, v], axis=0), preferred_element_type=F32)
        for u in range(2):
            lane = slice(u * FRADIX, (u + 1) * FRADIX)
            value = times((y[:FRADIX, lane], y[FRADIX:, lane]), (twist_ref[0], twist_ref[1]))
            at_rows = slice((2 * pair + u) * FRADIX, (2 * pair + u + 1) * FRADIX)
            for part in range(2):
                at_lane = slice(part * FRADIX, (part + 1) * FRADIX)
                high[at_rows, at_lane], low[at_rows, at_lane] = split_value(value[part])

    for pair in range(LEAD):
        turn_pair(pair)
    for pair in range(PACK // 2):
        if pair + LEAD < PACK // 2:
            turn_pair(pair + LEAD)
        at_rows = slice(pair * two, (pair + 1) * two)
        h, l = high[at_rows], low[at_rows]
        z = dot_nt(second_ref[...], jnp.concatenate([h, h, l], axis=1))
        for u in range(2):
            at = (2 * pair + u) * stride
            scratch[at : at + rows, :] = z[:, u * FRADIX : (u + 1) * FRADIX]
    channel_rows(n_gx, scratch, out_ref)


def whole(x):
    return pl.BlockSpec(x.shape, lambda *i: (0,) * x.ndim)


def spectra_call(volts, tables, n_gx, out_dev, start, stop):
    first, twist, second = tables
    per = 2 * FRADIX // out_dev
    second = second[start * per : stop * per]
    depth = 2 * AVG
    channels = stop - start
    inputs = volts.shape[0]
    return pl.pallas_call(
        functools.partial(spectra_kernel, n_gx),
        grid=(inputs // PACK,),
        in_specs=[
            pl.BlockSpec((PACK // PIECES, 2 * FRADIX, FRADIX), lambda i, p=p: (i * PIECES + p, 0, 0))
            for p in range(PIECES)
        ]
        + [whole(first), whole(twist), whole(second)],
        out_specs=pl.BlockSpec((n_gx, channels, PACK, depth), lambda i: (0, 0, i, 0)),
        out_shape=jax.ShapeDtypeStruct((n_gx, channels, inputs, depth), BF16),
        scratch_shapes=[
            pltpu.VMEM((PACK * FRADIX, 2 * FRADIX), BF16),
            pltpu.VMEM((PACK * FRADIX, 2 * FRADIX), BF16),
            pltpu.VMEM(((PACK + 1) * (channels * per + SUB), FRADIX), F32),
        ],
        name="spectra",
    )(*[volts] * PIECES, first, twist, second)


def correlate(x_ref, slot, vis, factor, unroll):
    sources, _, inputs, depth = x_ref.shape
    nin = sources * inputs
    half = depth // 2
    group = sources // 4
    panel = group * inputs

    def one(p, carry):
        base = pl.multiple_of(p * panel, panel)
        x = x_ref[pl.ds(p * group, group), slot].reshape(panel, depth)
        swapped = jnp.concatenate([x[:, half:], -x[:, :half]], axis=1)
        left = jnp.concatenate([x, swapped], axis=0)
        right = x_ref[:, slot].reshape(nin, depth)
        gram = (dot_nt(left, right) * factor).astype(BF16)
        for e in range(nin // BC):
            vis[0, e, pl.ds(base, panel), :] = gram[:panel, e * BC : (e + 1) * BC]
            vis[1, e, pl.ds(base, panel), :] = gram[panel:, e * BC : (e + 1) * BC]
        return carry

    lax.fori_loop(0, sources // group, one, 0, unroll=unroll)


def place_blocks(which, count_ref, list_ref, vis, grid):
    cells = grid.shape[1]
    wide = vis.shape[1]

    def place(s, carry):
        code = list_ref[which, s]
        cell = lax.rem(code, cells)
        block = lax.div(code, cells)
        e = lax.rem(block, wide)
        row = pl.multiple_of(lax.div(block, wide) * BR, BR)
        for part in range(2):
            grid[part, cell] += vis[part, e, pl.ds(row, BR), :].astype(F32)
        return carry

    lax.fori_loop(0, count_ref[which], place, 0)


LOADS = 8


def split_copies(source, target, sems):
    share = target.shape[1] // LOADS
    copies = []
    for i in range(LOADS):
        at = pl.ds(i * share, share)
        copies.append(pltpu.make_async_copy(source.at[:, at], target.at[:, at], sems.at[i]))
    return copies


def gram_kernel(slots, first_call, factor, count_ref, list_ref, *rest):
    x_refs, rest = rest[: len(slots)], rest[len(slots) :]
    out_ref, vis, grid, sems = rest[-4:]
    cells = grid.shape[1]
    if first_call:

        def clear(i, carry):
            grid[:, pl.ds(i * SUB, SUB)] = jnp.zeros((2, SUB, BR, BC), F32)
            return carry

        lax.fori_loop(0, cells // SUB, clear, 0)
    else:
        loads = split_copies(rest[0], grid, sems)
        for load in loads:
            load.start()
    which = 0
    for x_ref, many in zip(x_refs, slots):
        for slot in range(many):
            correlate(x_ref, slot, vis, factor, False)
            if which == 0 and not first_call:
                for load in loads:
                    load.wait()
            place_blocks(which, count_ref, list_ref, vis, grid)
            which += 1
    stores = split_copies(grid, out_ref, sems)
    for store in stores:
        store.start()
    for store in stores:
        store.wait()


def gram_call(counts, lists, streams, grid, cells, factor):
    first_call = grid is None
    shape = (2, cells, BR, BC)
    sources, _, inputs, depth = streams[0].shape
    nin = sources * inputs
    slots = tuple(x.shape[1] for x in streams)
    any_spec = pl.BlockSpec(memory_space=pl.ANY)
    vmem = pl.BlockSpec(memory_space=pltpu.VMEM)
    smem = pl.BlockSpec(memory_space=pltpu.SMEM)
    args = (counts, lists) + tuple(streams) + (() if first_call else (grid,))
    flops = sum(slots) * 4 * nin * nin * depth
    return pl.pallas_call(
        functools.partial(gram_kernel, slots, first_call, factor),
        in_specs=[smem, smem] + [vmem] * len(streams) + ([] if first_call else [any_spec]),
        out_specs=any_spec,
        out_shape=jax.ShapeDtypeStruct(shape, F32),
        scratch_shapes=[
            pltpu.VMEM((2, nin // BC, nin, BC), BF16),
            pltpu.VMEM(shape, F32),
            pltpu.SemaphoreType.DMA((LOADS,)),
        ],
        input_output_aliases={} if first_call else {2 + len(streams): 0},
        cost_estimate=pl.CostEstimate(flops=flops, transcendentals=0, bytes_accessed=2**24),
        name="gram",
    )(*args)


def row_block(block, grid, twist_ref, stage, turned):
    cols = TILE // BC
    inner = cols // 4
    for h in range(BR // SUB):
        rows = slice(h * SUB, (h + 1) * SUB)
        for q in range(4):
            at = [block * cols + 4 * m + q for m in range(inner)]
            values = butterflies([(grid[0, c, rows], grid[1, c, rows]) for c in at], 1.0)
            for k in range(inner):
                re, im = fixed_turn(values[k], q * k, cols, 1.0)
                stage[h, 0, q * inner + k] = re
                stage[h, 1, q * inner + k] = im
    for k in range(inner):
        halves_of = []
        for h in range(BR // SUB):
            values = [(stage[h, 0, q * inner + k], stage[h, 1, q * inner + k]) for q in range(4)]
            values = butterflies(values, 1.0)
            for m in range(4):
                at = k + m * inner
                if at:
                    factor = (twist_ref[0, at : at + 1, :], twist_ref[1, at : at + 1, :])
                    values[m] = times(values[m], factor)
            halves_of.append(values)
        for m in range(4):
            at = slice((k + m * inner) * BR, (k + m * inner + 1) * BR)
            for part in range(2):
                both = jnp.concatenate([values[m][part] for values in halves_of], axis=0)
                turned[block, at, part * BC : (part + 1) * BC] = both.astype(BF16)


SENDS = 4


def rows_kernel(
    factor,
    count_ref,
    list_ref,
    x_ref,
    grid_ref,
    twist_ref,
    second_ref,
    out_ref,
    vis,
    grid,
    stage,
    turned,
    scratch,
    ready,
    sems,
    out_sems,
):
    blocks = turned.shape[0]
    lanes = SUB * BR
    rows = 2 * BC
    step = pl.program_id(0)

    @pl.when(step == 0)
    def _():
        loads = split_copies(grid_ref, grid, sems)
        for load in loads:
            load.start()
        for slot in range(x_ref.shape[1]):
            correlate(x_ref, slot, vis, factor, True)
            if slot == 0:
                for load in loads:
                    load.wait()
            place_blocks(slot, count_ref, list_ref, vis, grid)

        def one(block, carry):
            row_block(block, grid, twist_ref, stage, turned)
            return carry

        lax.fori_loop(0, blocks, one, 0)

    stride = scratch.shape[0] // (blocks + 1)
    at_lane = pl.ds(pl.multiple_of(step * lanes, lanes), lanes)
    for b in range(blocks // 2):
        data = turned[2 * b : 2 * b + 2, at_lane].reshape(2 * lanes, rows)
        z = dot_nt(second_ref[...], data)
        for u in range(2):
            at = (2 * b + u) * stride
            scratch[at : at + rows, :] = z[:, u * lanes : (u + 1) * lanes]
    n_gx, lows, _, _ = out_ref.shape
    share = n_gx // SENDS

    def sends(at_step):
        slot = lax.rem(at_step, 2)
        at_out = pl.ds(pl.multiple_of(at_step * lanes, lanes), lanes)
        copies = []
        for i in range(SENDS):
            at = pl.ds(i * share, share)
            copies.append(pltpu.make_async_copy(ready.at[slot, at], out_ref.at[at, :, :, at_out], out_sems.at[slot, i]))
        return copies

    steps = pl.num_programs(0)
    slot = lax.rem(step, 2)

    @pl.when(step >= 2)
    def _():
        for copy in sends(step - 2):
            copy.wait()

    mine = sends(step)
    for d in range(n_gx):
        for k in range(lows):
            for part in range(2):
                row = (d * lows + k) * 2 + part
                piece = scratch[pl.ds(row, blocks, stride=stride), :]
                ready[slot, d, k, part * blocks : (part + 1) * blocks, :] = piece.astype(BF16)
        if d % share == share - 1:
            mine[d // share].start()

    @pl.when(step == steps - 1)
    def _():
        for at_step in (steps - 2, steps - 1):
            for copy in sends(at_step):
                copy.wait()


def rows_call(counts, lists, stream, grid, cells, factor, twist, second, n_gx):
    sources, _, inputs, _ = stream.shape
    nin = sources * inputs
    cols = TILE // BC
    blocks = cells // cols
    lanes = SUB * BR
    lows = BC // n_gx
    smem = pl.BlockSpec(memory_space=pltpu.SMEM)
    return pl.pallas_call(
        functools.partial(rows_kernel, factor),
        grid=(cols // SUB,),
        in_specs=[
            smem,
            smem,
            pl.BlockSpec(memory_space=pltpu.VMEM),
            pl.BlockSpec(memory_space=pltpu.HBM),
            whole(twist),
            whole(second),
        ],
        out_specs=pl.BlockSpec(memory_space=pltpu.HBM),
        out_shape=jax.ShapeDtypeStruct((n_gx, lows, 2 * blocks, cols * BR), BF16),
        scratch_shapes=[
            pltpu.VMEM((2, nin // BC, nin, BC), BF16),
            pltpu.VMEM((2, cells, BR, BC), F32),
            pltpu.VMEM((BR // SUB, 2, cols, SUB, BC), F32),
            pltpu.VMEM((blocks, cols * BR, 2 * BC), BF16),
            pltpu.VMEM(((blocks + 1) * (2 * BC + SUB), lanes), F32),
            pltpu.VMEM((2, n_gx, lows, 2 * blocks, lanes), BF16),
            pltpu.SemaphoreType.DMA((LOADS,)),
            pltpu.SemaphoreType.DMA((2, SENDS)),
        ],
        compiler_params=pltpu.CompilerParams(vmem_limit_bytes=48 * 2**20),
        name="rows",
    )(counts, lists, stream, grid, twist, second)


def column_kernel(data_ref, first_ref, cos_ref, sin_ref, out_ref, scratch, ready, out_sems):
    n_gx, _, rows, lanes = data_ref.shape
    count = TILE // BR
    span = SUB * BR

    def mix(g):
        data = data_ref[:, 0, :, g * span : (g + 1) * span].reshape(n_gx * rows, span)
        mixed = dot_tn(data, first_ref[...])
        for b in range(2 * count // BC):
            scratch[g, b * span : (b + 1) * span, :] = mixed[:, b * BC : (b + 1) * BC]

    step = pl.program_id(0)
    steps = pl.num_programs(0)
    slot = lax.rem(step, 2)
    groups = lanes // (SUB * BR)

    def sends(at_step):
        at_slot = lax.rem(at_step, 2)
        copies = []
        for g in range(groups):
            at = pl.ds(g * SUB, SUB)
            for part in range(2):
                source, target = ready.at[at_slot, part, at], out_ref.at[part, at_step, at]
                copies.append(pltpu.make_async_copy(source, target, out_sems.at[at_slot, 2 * g + part]))
        return copies

    @pl.when(step >= 2)
    def _():
        for copy in sends(step - 2):
            copy.wait()

    mine = sends(step)
    mix(0)
    for g in range(groups):
        if g + 1 < groups:
            mix(g + 1)
        for b in range(count // BC):
            lane = slice(b * BC, (b + 1) * BC)
            values = []
            for r in range(BR):
                value = (
                    scratch[g, pl.ds(b * span + r, SUB, stride=BR), :],
                    scratch[g, pl.ds((count // BC + b) * span + r, SUB, stride=BR), :],
                )
                factor = (cos_ref[r : r + 1, lane], sin_ref[r : r + 1, lane])
                values.append(times(value, factor) if r else value)
            values = butterflies(values, 1.0)
            for k in range(BR):
                at = slice(k * count + b * BC, k * count + (b + 1) * BC)
                for part in range(2):
                    ready[slot, part, g * SUB : (g + 1) * SUB, at] = values[k][part]
        mine[2 * g].start()
        mine[2 * g + 1].start()

    @pl.when(step == steps - 1)
    def _():
        for at_step in (steps - 2, steps - 1):
            for copy in sends(at_step):
                copy.wait()


def column_call(data, first, cos, sin):
    n_gx, lows, rows, lanes = data.shape
    cols = TILE // BC
    return pl.pallas_call(
        column_kernel,
        grid=(lows,),
        in_specs=[
            pl.BlockSpec((n_gx, 1, rows, lanes), lambda i: (0, i, 0, 0)),
            whole(first),
            whole(cos),
            whole(sin),
        ],
        out_specs=pl.BlockSpec(memory_space=pl.ANY),
        out_shape=jax.ShapeDtypeStruct((2, lows, cols, TILE), F32),
        scratch_shapes=[
            pltpu.VMEM((cols // SUB, (2 * (TILE // BR) // BC + 1) * SUB * BR, BC), F32),
            pltpu.VMEM((2, 2, cols, TILE), F32),
            pltpu.SemaphoreType.DMA((2, 2 * cols // SUB)),
        ],
        name="column",
    )(data, first, cos, sin)


def work_lists(tile_of, cell_of, me, out_dev, cells):
    groups, blocks = tile_of.shape
    per = blocks // out_dev
    taken = (tile_of == me).reshape(groups, out_dev, per)
    number = taken.astype(jnp.int32)
    rank = jnp.cumsum(number, axis=2) - number
    slot = jnp.where(taken, rank, -1)
    code = jnp.arange(per, dtype=jnp.int32) * cells + cell_of.reshape(groups, out_dev, per)
    hit = jnp.arange(per, dtype=jnp.int32)[:, None] == slot[:, :, None, :]
    lists = jnp.sum(jnp.where(hit, code[:, :, None, :], 0), axis=3)
    return jnp.sum(number, axis=2), lists


def pair_plan(voltages, tile_of, cell_of):
    n_gx = lax.axis_size("gx")
    _, st_dev, pols, spectra, _, fine = voltages.shape
    inputs = st_dev * pols
    out_dev = fine // (n_gx * AVG)
    cells = (TILE // n_gx // BR) * (TILE // BC)
    me = lax.axis_index("grp")
    counts, lists = work_lists(tile_of, cell_of, me, out_dev, cells)
    swap = jnp.where(me == 0, jnp.arange(2), jnp.arange(2)[::-1])
    counts, lists = jnp.take(counts, swap, axis=0), jnp.take(lists, swap, axis=0)

    volts = voltages.reshape(inputs, 2, FRADIX, FRADIX).transpose(0, 2, 1, 3)
    volts = volts.reshape(inputs, 2 * FRADIX, FRADIX)
    factor = 1.0 / math.sqrt(spectra * AVG)
    tables = spectra_tables(n_gx, out_dev)
    front, middle, last = 0, out_dev // 2, out_dev - 1

    def exchange(spec):
        return lax.all_to_all(spec, "gx", split_axis=0, concat_axis=0, tiled=True)

    def swap_groups(data):
        return lax.ppermute(data, "grp", [(0, 1), (1, 0)])

    def work(grid, *items):
        number = jnp.concatenate([counts[g, start:stop] for g, start, stop, _ in items])
        list_of = jnp.concatenate([lists[g, start:stop] for g, start, stop, _ in items])
        streams = [data for _, _, _, data in items]
        return gram_call(number, list_of, streams, grid, cells, factor)

    spec_a = spectra_call(volts, tables, n_gx, out_dev, front, middle)
    mine_a = exchange(spec_a)
    spec_c = spectra_call(volts, tables, n_gx, out_dev, last, out_dev)
    other_c = swap_groups(spec_c)
    spec_b = spectra_call(volts, tables, n_gx, out_dev, middle, last)
    other_a = swap_groups(mine_a)
    mine_b = exchange(spec_b)
    grid = work(None, (0, front, middle, mine_a))
    other_b = swap_groups(mine_b)
    both_c = exchange(jnp.concatenate([spec_c, other_c], axis=1))
    grid = work(grid, (0, middle, last, mine_b), (1, front, middle, other_a))
    grid = work(grid, (1, middle, last, other_b))
    twist, second = row_tables()
    rows = rows_call(counts[:, last], lists[:, last], both_c, grid, cells, factor, twist, second, n_gx)
    data = exchange(rows)
    cos, sin = column_twist()
    image = column_call(data, column_tables(n_gx), cos, sin)
    return image.reshape(1, 2, TILE // n_gx, TILE)


def base_table(radix, sign):
    index = jnp.arange(radix, dtype=jnp.int32)
    product = index[:, None] * index[None, :] % radix
    angle = sign * 2.0 * math.pi / radix * product.astype(jnp.float32)
    return (jnp.cos(angle), jnp.sin(angle))


def twist_table(radix, sign):
    index = jnp.arange(radix, dtype=jnp.int32)
    product = index[:, None] * index[None, :]
    angle = sign * 2.0 * math.pi / (radix * radix) * product.astype(jnp.float32)
    return (jnp.cos(angle), jnp.sin(angle))


def complex_einsum(form, table, real_part, imag_part):
    cos_part, sin_part = table

    def product(left, right):
        return jnp.einsum(form, left, right, precision=lax.Precision.HIGH)

    new_real = product(cos_part, real_part) - product(sin_part, imag_part)
    new_imag = product(cos_part, imag_part) + product(sin_part, real_part)
    return (new_real, new_imag)


def fourier(real_part, imag_part, radix, sign, to_front):
    count = real_part.shape[0]
    real_part = real_part.reshape(count, radix, radix)
    imag_part = imag_part.reshape(count, radix, radix)
    table = base_table(radix, sign)
    real_part, imag_part = complex_einsum("ak,rab->rkb", table, real_part, imag_part)
    twist_cos, twist_sin = twist_table(radix, sign)
    twist_cos = twist_cos.T
    twist_sin = twist_sin.T
    turned_real = real_part * twist_cos - imag_part * twist_sin
    turned_imag = real_part * twist_sin + imag_part * twist_cos
    if to_front:
        form = "bj,rkb->jkr"
        shape = (radix * radix, count)
    else:
        form = "bj,rkb->rjk"
        shape = (count, radix * radix)
    out_real, out_imag = complex_einsum(form, table, turned_real, turned_imag)
    return (out_real.reshape(shape) / radix, out_imag.reshape(shape) / radix)


def operands(local):
    stations, pols, spectra, _, channels = local.shape
    inputs = stations * pols
    nout = channels // AVG
    grouped = local.reshape(inputs, spectra, 2, nout, AVG).transpose(3, 0, 1, 2, 4)
    swapped = jnp.stack([grouped[:, :, :, 1], -grouped[:, :, :, 0]], axis=3)
    left = jnp.stack([grouped, swapped], axis=1).reshape(nout, 2 * inputs, spectra, 2 * AVG)
    right = grouped.reshape(nout, inputs, spectra, 2 * AVG)
    return (left, right)


def gram_all(local):
    left, right = operands(local)
    nout, rows_two, spectra, depth = left.shape
    left = left.reshape(nout, rows_two, spectra * depth)
    right = right.reshape(nout, rows_two // 2, spectra * depth)
    return jnp.einsum("oyk,ork->oyr", left, right, preferred_element_type=jnp.float32)


def pair_fits(gx_count, shape):
    lead, st_dev, pols, spectra, _, fine = shape
    return (
        lead == 1
        and spectra == 1
        and fine == FRADIX * FRADIX
        and (st_dev * pols) % PACK == 0
        and fine % (gx_count * AVG) == 0
        and TILE // gx_count // BR == PACK
        and fine // (gx_count * AVG) >= 4
        and gx_count % 4 == 0
    )


def on_device(voltages, tile_of, cell_of):
    grp_count = lax.axis_size("grp")
    gx_count = lax.axis_size("gx")
    _, st_dev, pols, spectra, _, fine = voltages.shape
    if grp_count == 2 and pair_fits(gx_count, voltages.shape):
        return pair_plan(voltages, tile_of, cell_of)
    volts = voltages.reshape(st_dev * pols * spectra, 2, fine).astype(jnp.float32)
    spec_re, spec_im = fourier(volts[:, 0], volts[:, 1], FRADIX, -1.0, False)
    spec = jnp.stack([spec_re, spec_im], axis=1).astype(jnp.bfloat16)
    spec = spec.reshape(st_dev, pols, spectra, 2, fine)
    local = lax.all_to_all(spec, "gx", split_axis=4, concat_axis=0, tiled=True)
    gram = gram_all(local)
    factor = 1.0 / math.sqrt(spectra * AVG)
    out_dev = gram.shape[0]
    inputs = gram.shape[2]
    vis = (gram * factor).astype(jnp.bfloat16).reshape(out_dev, 2, inputs, inputs)
    width = 2 * BR * BC
    shaped = vis.reshape(out_dev, 2, inputs // BR, BR, inputs // BC, BC)
    blocks = shaped.transpose(0, 2, 4, 1, 3, 5).reshape(-1, width)
    count_blocks = blocks.shape[0]
    capacity = max(2, count_blocks // (4 * grp_count))
    slots = grp_count * capacity
    me = lax.axis_index("grp")
    groups = tile_of.shape[0]
    marked = (tile_of[:, None, :] == jnp.arange(grp_count, dtype=jnp.int32)[None, :, None]).astype(
        jnp.int32
    )
    rank_all = jnp.sum((jnp.cumsum(marked, axis=2) - marked) * marked, axis=1)
    my_tiles = lax.dynamic_index_in_dim(tile_of, me, 0, keepdims=False)
    my_rank = lax.dynamic_index_in_dim(rank_all, me, 0, keepdims=False)
    slot_id = jnp.where(my_tiles < 0, -1, my_tiles * capacity + my_rank)
    hits = jnp.arange(slots, dtype=jnp.int32)[:, None] == slot_id[None, :]
    filled = jnp.any(hits, axis=1)
    source = jnp.where(filled, jnp.argmax(hits, axis=1), count_blocks)
    padded = jnp.concatenate([blocks, jnp.zeros((1, width), jnp.bfloat16)], axis=0)
    outgoing = jnp.take(padded, source, axis=0)
    outgoing = outgoing.reshape(grp_count, capacity, width)
    arrived = lax.all_to_all(outgoing, "grp", split_axis=0, concat_axis=0, tiled=True)
    slab = TILE // gx_count
    row_blocks = slab // BR
    col_blocks = TILE // BC
    cells_count = row_blocks * col_blocks
    source_group = jnp.arange(groups, dtype=jnp.int32)[:, None]
    slot_flat = jnp.where(tile_of == me, source_group * capacity + rank_all, -1).reshape(-1)
    cell_flat = cell_of.reshape(-1)
    cell_hit = (jnp.arange(cells_count, dtype=jnp.int32)[:, None] == cell_flat[None, :]).astype(
        jnp.bfloat16
    )
    slot_hit = (jnp.arange(slots, dtype=jnp.int32)[:, None] == slot_flat[None, :]).astype(
        jnp.bfloat16
    )
    place = lax.dot_general(
        cell_hit, slot_hit, (((1,), (1,)), ((), ())), preferred_element_type=jnp.float32
    )
    place = place.astype(jnp.bfloat16)
    grid = jnp.dot(place, arrived.reshape(slots, width), preferred_element_type=jnp.float32)
    grid = (
        grid.reshape(row_blocks, col_blocks, 2, BR, BC)
        .transpose(2, 0, 3, 1, 4)
        .reshape(2, slab, TILE)
    )
    rows_re, rows_im = fourier(grid[0], grid[1], TRADIX, 1.0, True)
    rows = jnp.stack([rows_re, rows_im], axis=0).astype(jnp.bfloat16)
    columns = lax.all_to_all(rows, "gx", split_axis=1, concat_axis=2, tiled=True)
    kx_local = columns.shape[1]
    image_re, image_im = fourier(
        columns[0].astype(jnp.float32), columns[1].astype(jnp.float32), TRADIX, 1.0, False
    )
    image = jnp.stack([image_re, image_im], axis=0).reshape(1, 2, kx_local, TILE)
    return image


def solution(mesh):
    in_specs = (P("grp", "gx", None, None, None, None), P(None, "gx"), P(None, "gx"))
    out_specs = P("grp", None, "gx", None)
    return jax.shard_map(
        on_device, mesh=mesh, in_specs=in_specs, out_specs=out_specs, check_vma=False
    )
```

```python
import functools
import math

import jax
import jax.numpy as jnp
import numpy as np
from jax import lax
from jax.experimental import pallas as pl
from jax.experimental.pallas import tpu as pltpu
from jax.sharding import PartitionSpec as P


FRADIX = 128
AVG = 256
BR = 16
BC = 128
TRADIX = 64
TILE = 4096
SUB = 8
PACK = 16
F32 = jnp.float32
BF16 = jnp.bfloat16


def halves(matrix):
    high = matrix.astype(np.float32).astype(BF16)
    low = (matrix - high.astype(np.float64)).astype(np.float32).astype(BF16)
    return high, low


def complex_table(angle, scale):
    cos, sin = scale * np.cos(angle), scale * np.sin(angle)
    return np.stack([np.stack([cos, -sin]), np.stack([sin, cos])])


def turn(product, period, sign):
    return sign * 2.0 * np.pi / period * (product % period)


def spectra_tables(n_gx, out_dev):
    index = np.arange(FRADIX)
    first = complex_table(turn(np.outer(index, index), FRADIX, -1.0), 1.0 / FRADIX)
    first = first.transpose(0, 2, 3, 1).reshape(2 * FRADIX, 2 * FRADIX)
    high, low = halves(first)
    first = np.concatenate([high, low], axis=1)
    angle = turn(np.outer(index, index), FRADIX * FRADIX, -1.0)
    twist = np.stack([np.cos(angle), np.sin(angle)]).astype(np.float32)
    second = complex_table(turn(np.outer(index, index), FRADIX, -1.0), 1.0)
    low_count = FRADIX // (n_gx * out_dev)
    second = second.reshape(2, 2, n_gx, out_dev, low_count, FRADIX)
    second = second.transpose(3, 2, 0, 4, 1, 5).reshape(2 * FRADIX, 2 * FRADIX)
    high, low = halves(second)
    second = np.concatenate([high, low, high], axis=1)
    return first, twist, second


def row_tables():
    cols = TILE // BC
    k1, w = np.arange(cols), np.arange(BC)
    angle = turn(np.outer(k1, w), TILE, 1.0)
    twist = np.stack([np.cos(angle), np.sin(angle)]).astype(np.float32)
    second = complex_table(turn(np.outer(w, w), BC, 1.0), 1.0 / math.sqrt(TILE))
    second = second.transpose(2, 0, 1, 3).reshape(2 * BC, 2 * BC)
    return twist, halves(second)[0]


def column_tables(n_gx):
    count = TILE // BR
    blocks = count // n_gx
    index = np.arange(count)
    first = complex_table(turn(np.outer(index, index), count, 1.0), 1.0 / math.sqrt(TILE))
    first = first.reshape(2, 2, n_gx, blocks, count)
    first = first.transpose(2, 1, 3, 0, 4).reshape(2 * count, 2 * count)
    return halves(first)[0]


def column_twist():
    shape = (BR, TILE // BR)
    product = lax.broadcasted_iota(jnp.int32, shape, 0) * lax.broadcasted_iota(jnp.int32, shape, 1)
    angle = 2.0 * math.pi / TILE * product.astype(F32)
    return jnp.cos(angle), jnp.sin(angle)


def times(value, factor):
    re, im = value
    c, s = factor
    return (re * c - im * s, re * s + im * c)


def fixed_turn(value, step, count, sign):
    re, im = value
    step = step % count
    if step == 0:
        return value
    if 4 * step == count:
        return (-im, re) if sign > 0 else (im, -re)
    angle = sign * 2.0 * math.pi * step / count
    c, s = math.cos(angle), math.sin(angle)
    if 8 * step == count:
        return ((re - im) * c, (re + im) * c) if sign > 0 else ((re + im) * c, (im - re) * c)
    if 8 * step == 3 * count:
        h = abs(c)
        return ((-re - im) * h, (re - im) * h) if sign > 0 else ((im - re) * h, (-re - im) * h)
    return (re * c - im * s, re * s + im * c)


def butterflies(values, sign):
    count = len(values)
    if count == 1:
        return values
    even = butterflies(values[0::2], sign)
    odd = butterflies(values[1::2], sign)
    out = [None] * count
    for k in range(count // 2):
        turned = fixed_turn(odd[k], k, count, sign)
        out[k] = (even[k][0] + turned[0], even[k][1] + turned[1])
        out[k + count // 2] = (even[k][0] - turned[0], even[k][1] - turned[1])
    return out


def split_value(value):
    high = value.astype(BF16)
    return high, (value - high.astype(F32)).astype(BF16)


def dot_nt(left, right):
    return lax.dot_general(left, right, (((1,), (1,)), ((), ())), preferred_element_type=F32)


def dot_tn(left, right):
    return lax.dot_general(left, right, (((0,), (0,)), ((), ())), preferred_element_type=F32)


def channel_rows(n_gx, scratch, out_ref):
    stride = scratch.shape[0] // (PACK + 1)
    channels = out_ref.shape[1]
    per = out_ref.shape[3] // FRADIX
    for o in range(channels):
        for d in range(n_gx):
            for t in range(per):
                piece = scratch[pl.ds((o * n_gx + d) * per + t, PACK, stride=stride), :]
                out_ref[d, o, :, t * FRADIX : (t + 1) * FRADIX] = piece.astype(BF16)


PIECES = 4
LEAD = 4


def spectra_kernel(n_gx, *refs):
    v_refs, (first_ref, twist_ref, second_ref, out_ref, high, low, scratch) = refs[:PIECES], refs[PIECES:]
    rows = second_ref.shape[0]
    stride = scratch.shape[0] // (PACK + 1)
    two = 2 * FRADIX
    share = PACK // PIECES

    def turn_pair(pair):
        v_ref, at = v_refs[2 * pair // share], 2 * pair % share
        v = jnp.concatenate([v_ref[at], v_ref[at + 1]], axis=1)
        y = jnp.dot(first_ref[...], jnp.concatenate([v, v], axis=0), preferred_element_type=F32)
        for u in range(2):
            lane = slice(u * FRADIX, (u + 1) * FRADIX)
            value = times((y[:FRADIX, lane], y[FRADIX:, lane]), (twist_ref[0], twist_ref[1]))
            at_rows = slice((2 * pair + u) * FRADIX, (2 * pair + u + 1) * FRADIX)
            for part in range(2):
                at_lane = slice(part * FRADIX, (part + 1) * FRADIX)
                high[at_rows, at_lane], low[at_rows, at_lane] = split_value(value[part])

    for pair in range(LEAD):
        turn_pair(pair)
    for pair in range(PACK // 2):
        if pair + LEAD < PACK // 2:
            turn_pair(pair + LEAD)
        at_rows = slice(pair * two, (pair + 1) * two)
        h, l = high[at_rows], low[at_rows]
        z = dot_nt(second_ref[...], jnp.concatenate([h, h, l], axis=1))
        for u in range(2):
            at = (2 * pair + u) * stride
            scratch[at : at + rows, :] = z[:, u * FRADIX : (u + 1) * FRADIX]
    channel_rows(n_gx, scratch, out_ref)


def whole(x):
    return pl.BlockSpec(x.shape, lambda *i: (0,) * x.ndim)


def spectra_call(volts, tables, n_gx, out_dev, start, stop):
    first, twist, second = tables
    per = 2 * FRADIX // out_dev
    second = second[start * per : stop * per]
    depth = 2 * AVG
    channels = stop - start
    inputs = volts.shape[0]
    return pl.pallas_call(
        functools.partial(spectra_kernel, n_gx),
        grid=(inputs // PACK,),
        in_specs=[
            pl.BlockSpec((PACK // PIECES, 2 * FRADIX, FRADIX), lambda i, p=p: (i * PIECES + p, 0, 0))
            for p in range(PIECES)
        ]
        + [whole(first), whole(twist), whole(second)],
        out_specs=pl.BlockSpec((n_gx, channels, PACK, depth), lambda i: (0, 0, i, 0)),
        out_shape=jax.ShapeDtypeStruct((n_gx, channels, inputs, depth), BF16),
        scratch_shapes=[
            pltpu.VMEM((PACK * FRADIX, 2 * FRADIX), BF16),
            pltpu.VMEM((PACK * FRADIX, 2 * FRADIX), BF16),
            pltpu.VMEM(((PACK + 1) * (channels * per + SUB), FRADIX), F32),
        ],
        name="spectra",
    )(*[volts] * PIECES, first, twist, second)


def correlate(x_ref, slot, vis, factor, unroll):
    sources, _, inputs, depth = x_ref.shape
    nin = sources * inputs
    half = depth // 2
    group = sources // 4
    panel = group * inputs

    def one(p, carry):
        base = pl.multiple_of(p * panel, panel)
        x = x_ref[pl.ds(p * group, group), slot].reshape(panel, depth)
        swapped = jnp.concatenate([x[:, half:], -x[:, :half]], axis=1)
        left = jnp.concatenate([x, swapped], axis=0)
        right = x_ref[:, slot].reshape(nin, depth)
        gram = (dot_nt(left, right) * factor).astype(BF16)
        for e in range(nin // BC):
            vis[0, e, pl.ds(base, panel), :] = gram[:panel, e * BC : (e + 1) * BC]
            vis[1, e, pl.ds(base, panel), :] = gram[panel:, e * BC : (e + 1) * BC]
        return carry

    lax.fori_loop(0, sources // group, one, 0, unroll=unroll)


def parts_of(number, size):
    if size & (size - 1):
        return lax.div(number, size), lax.rem(number, size)
    return lax.shift_right_logical(number, size.bit_length() - 1), number & (size - 1)


def place_blocks(which, count_ref, list_ref, vis, grid):
    cells = grid.shape[1]
    wide = vis.shape[1]

    def place(s, carry):
        code = list_ref[which, s]
        block, cell = parts_of(code, cells)
        high, e = parts_of(block, wide)
        row = pl.multiple_of(high * BR, BR)
        for part in range(2):
            grid[part, cell] += vis[part, e, pl.ds(row, BR), :].astype(F32)
        return carry

    lax.fori_loop(0, count_ref[which], place, 0)


LOADS = 8


def split_copies(source, target, sems):
    share = target.shape[1] // LOADS
    copies = []
    for i in range(LOADS):
        at = pl.ds(i * share, share)
        copies.append(pltpu.make_async_copy(source.at[:, at], target.at[:, at], sems.at[i]))
    return copies


def gram_kernel(slots, first_call, factor, count_ref, list_ref, *rest):
    x_refs, rest = rest[: len(slots)], rest[len(slots) :]
    out_ref, vis, grid, sems = rest[-4:]
    cells = grid.shape[1]
    if first_call:

        def clear(i, carry):
            grid[:, pl.ds(i * SUB, SUB)] = jnp.zeros((2, SUB, BR, BC), F32)
            return carry

        lax.fori_loop(0, cells // SUB, clear, 0)
    else:
        loads = split_copies(rest[0], grid, sems)
        for load in loads:
            load.start()
    which = 0
    for x_ref, many in zip(x_refs, slots):
        for slot in range(many):
            correlate(x_ref, slot, vis, factor, False)
            if which == 0 and not first_call:
                for load in loads:
                    load.wait()
            place_blocks(which, count_ref, list_ref, vis, grid)
            which += 1
    stores = split_copies(grid, out_ref, sems)
    for store in stores:
        store.start()
    for store in stores:
        store.wait()


def gram_call(counts, lists, streams, grid, cells, factor):
    first_call = grid is None
    shape = (2, cells, BR, BC)
    sources, _, inputs, depth = streams[0].shape
    nin = sources * inputs
    slots = tuple(x.shape[1] for x in streams)
    any_spec = pl.BlockSpec(memory_space=pl.ANY)
    vmem = pl.BlockSpec(memory_space=pltpu.VMEM)
    smem = pl.BlockSpec(memory_space=pltpu.SMEM)
    args = (counts, lists) + tuple(streams) + (() if first_call else (grid,))
    flops = sum(slots) * 4 * nin * nin * depth
    return pl.pallas_call(
        functools.partial(gram_kernel, slots, first_call, factor),
        in_specs=[smem, smem] + [vmem] * len(streams) + ([] if first_call else [any_spec]),
        out_specs=any_spec,
        out_shape=jax.ShapeDtypeStruct(shape, F32),
        scratch_shapes=[
            pltpu.VMEM((2, nin // BC, nin, BC), BF16),
            pltpu.VMEM(shape, F32),
            pltpu.SemaphoreType.DMA((LOADS,)),
        ],
        input_output_aliases={} if first_call else {2 + len(streams): 0},
        cost_estimate=pl.CostEstimate(flops=flops, transcendentals=0, bytes_accessed=2**24),
        name="gram",
    )(*args)


def row_block(block, grid, twist_ref, stage, turned):
    cols = TILE // BC
    inner = cols // 4
    for h in range(BR // SUB):
        rows = slice(h * SUB, (h + 1) * SUB)
        for q in range(4):
            at = [block * cols + 4 * m + q for m in range(inner)]
            values = butterflies([(grid[0, c, rows], grid[1, c, rows]) for c in at], 1.0)
            for k in range(inner):
                re, im = fixed_turn(values[k], q * k, cols, 1.0)
                stage[h, 0, q * inner + k] = re
                stage[h, 1, q * inner + k] = im
    for k in range(inner):
        halves_of = []
        for h in range(BR // SUB):
            values = [(stage[h, 0, q * inner + k], stage[h, 1, q * inner + k]) for q in range(4)]
            values = butterflies(values, 1.0)
            for m in range(4):
                at = k + m * inner
                if at:
                    factor = (twist_ref[0, at : at + 1, :], twist_ref[1, at : at + 1, :])
                    values[m] = times(values[m], factor)
            halves_of.append(values)
        for m in range(4):
            at = slice((k + m * inner) * BR, (k + m * inner + 1) * BR)
            for part in range(2):
                both = jnp.concatenate([values[m][part] for values in halves_of], axis=0)
                turned[block, at, part * BC : (part + 1) * BC] = both.astype(BF16)


SENDS = 4


def rows_kernel(
    factor,
    count_ref,
    list_ref,
    x_ref,
    grid_ref,
    twist_ref,
    second_ref,
    out_ref,
    vis,
    grid,
    stage,
    turned,
    scratch,
    ready,
    sems,
    out_sems,
):
    blocks = turned.shape[0]
    lanes = SUB * BR
    rows = 2 * BC
    step = pl.program_id(0)

    @pl.when(step == 0)
    def _():
        loads = split_copies(grid_ref, grid, sems)
        for load in loads:
            load.start()
        for slot in range(x_ref.shape[1]):
            correlate(x_ref, slot, vis, factor, True)
            if slot == 0:
                for load in loads:
                    load.wait()
            place_blocks(slot, count_ref, list_ref, vis, grid)

        def one(block, carry):
            row_block(block, grid, twist_ref, stage, turned)
            return carry

        lax.fori_loop(0, blocks, one, 0)

    stride = scratch.shape[0] // (blocks + 1)
    at_lane = pl.ds(pl.multiple_of(step * lanes, lanes), lanes)
    for b in range(blocks // 2):
        data = turned[2 * b : 2 * b + 2, at_lane].reshape(2 * lanes, rows)
        z = dot_nt(second_ref[...], data)
        for u in range(2):
            at = (2 * b + u) * stride
            scratch[at : at + rows, :] = z[:, u * lanes : (u + 1) * lanes]
    n_gx, lows, _, _ = out_ref.shape
    share = n_gx // SENDS

    def sends(at_step):
        slot = lax.rem(at_step, 2)
        at_out = pl.ds(pl.multiple_of(at_step * lanes, lanes), lanes)
        copies = []
        for i in range(SENDS):
            at = pl.ds(i * share, share)
            copies.append(pltpu.make_async_copy(ready.at[slot, at], out_ref.at[at, :, :, at_out], out_sems.at[slot, i]))
        return copies

    steps = pl.num_programs(0)
    slot = lax.rem(step, 2)

    @pl.when(step >= 2)
    def _():
        for copy in sends(step - 2):
            copy.wait()

    mine = sends(step)
    for d in range(n_gx):
        for k in range(lows):
            for part in range(2):
                row = (d * lows + k) * 2 + part
                piece = scratch[pl.ds(row, blocks, stride=stride), :]
                ready[slot, d, k, part * blocks : (part + 1) * blocks, :] = piece.astype(BF16)
        if d % share == share - 1:
            mine[d // share].start()

    @pl.when(step == steps - 1)
    def _():
        for at_step in (steps - 2, steps - 1):
            for copy in sends(at_step):
                copy.wait()


def rows_call(counts, lists, stream, grid, cells, factor, twist, second, n_gx):
    sources, _, inputs, _ = stream.shape
    nin = sources * inputs
    cols = TILE // BC
    blocks = cells // cols
    lanes = SUB * BR
    lows = BC // n_gx
    smem = pl.BlockSpec(memory_space=pltpu.SMEM)
    return pl.pallas_call(
        functools.partial(rows_kernel, factor),
        grid=(cols // SUB,),
        in_specs=[
            smem,
            smem,
            pl.BlockSpec(memory_space=pltpu.VMEM),
            pl.BlockSpec(memory_space=pltpu.HBM),
            whole(twist),
            whole(second),
        ],
        out_specs=pl.BlockSpec(memory_space=pltpu.HBM),
        out_shape=jax.ShapeDtypeStruct((n_gx, lows, 2 * blocks, cols * BR), BF16),
        scratch_shapes=[
            pltpu.VMEM((2, nin // BC, nin, BC), BF16),
            pltpu.VMEM((2, cells, BR, BC), F32),
            pltpu.VMEM((BR // SUB, 2, cols, SUB, BC), F32),
            pltpu.VMEM((blocks, cols * BR, 2 * BC), BF16),
            pltpu.VMEM(((blocks + 1) * (2 * BC + SUB), lanes), F32),
            pltpu.VMEM((2, n_gx, lows, 2 * blocks, lanes), BF16),
            pltpu.SemaphoreType.DMA((LOADS,)),
            pltpu.SemaphoreType.DMA((2, SENDS)),
        ],
        compiler_params=pltpu.CompilerParams(vmem_limit_bytes=48 * 2**20),
        name="rows",
    )(counts, lists, stream, grid, twist, second)


def column_kernel(data_a, data_b, data_c, data_d, first_ref, cos_ref, sin_ref, out_ref, scratch, ready, out_sems):
    pieces = (data_a, data_b, data_c, data_d)
    share, _, rows, lanes = data_a.shape
    count = TILE // BR
    span = SUB * BR

    def mix(g):
        at = slice(g * span, (g + 1) * span)
        data = jnp.concatenate([x[:, 0, :, at].reshape(share * rows, span) for x in pieces], axis=0)
        mixed = dot_tn(data, first_ref[...])
        for b in range(2 * count // BC):
            scratch[g, b * span : (b + 1) * span, :] = mixed[:, b * BC : (b + 1) * BC]

    step = pl.program_id(0)
    steps = pl.num_programs(0)
    slot = lax.rem(step, 2)
    groups = lanes // (SUB * BR)

    def sends(at_step):
        at_slot = lax.rem(at_step, 2)
        copies = []
        for g in range(groups):
            at = pl.ds(g * SUB, SUB)
            for part in range(2):
                source, target = ready.at[at_slot, part, at], out_ref.at[part, at_step, at]
                copies.append(pltpu.make_async_copy(source, target, out_sems.at[at_slot, 2 * g + part]))
        return copies

    @pl.when(step >= 2)
    def _():
        for copy in sends(step - 2):
            copy.wait()

    mine = sends(step)
    mix(0)
    for g in range(groups):
        if g + 1 < groups:
            mix(g + 1)
        for b in range(count // BC):
            lane = slice(b * BC, (b + 1) * BC)
            values = []
            for r in range(BR):
                value = (
                    scratch[g, pl.ds(b * span + r, SUB, stride=BR), :],
                    scratch[g, pl.ds((count // BC + b) * span + r, SUB, stride=BR), :],
                )
                factor = (cos_ref[r : r + 1, lane], sin_ref[r : r + 1, lane])
                values.append(times(value, factor) if r else value)
            values = butterflies(values, 1.0)
            for k in range(BR):
                at = slice(k * count + b * BC, k * count + (b + 1) * BC)
                for part in range(2):
                    ready[slot, part, g * SUB : (g + 1) * SUB, at] = values[k][part]
        mine[2 * g].start()
        mine[2 * g + 1].start()

    @pl.when(step == steps - 1)
    def _():
        for at_step in (steps - 2, steps - 1):
            for copy in sends(at_step):
                copy.wait()


def column_call(data, first, cos, sin):
    n_gx, lows, rows, lanes = data.shape
    cols = TILE // BC
    return pl.pallas_call(
        column_kernel,
        grid=(lows,),
        in_specs=[
            *[pl.BlockSpec((n_gx // 4, 1, rows, lanes), lambda i, p=p: (p, i, 0, 0)) for p in range(4)],
            whole(first),
            whole(cos),
            whole(sin),
        ],
        out_specs=pl.BlockSpec(memory_space=pl.ANY),
        out_shape=jax.ShapeDtypeStruct((2, lows, cols, TILE), F32),
        scratch_shapes=[
            pltpu.VMEM((cols // SUB, (2 * (TILE // BR) // BC + 1) * SUB * BR, BC), F32),
            pltpu.VMEM((2, 2, cols, TILE), F32),
            pltpu.SemaphoreType.DMA((2, 2 * cols // SUB)),
        ],
        name="column",
    )(data, data, data, data, first, cos, sin)


def work_lists(tile_of, cell_of, me, out_dev, cells):
    groups, blocks = tile_of.shape
    per = blocks // out_dev
    taken = (tile_of == me).reshape(groups, out_dev, per)
    number = taken.astype(jnp.int32)
    rank = jnp.cumsum(number, axis=2) - number
    slot = jnp.where(taken, rank, -1)
    code = jnp.arange(per, dtype=jnp.int32) * cells + cell_of.reshape(groups, out_dev, per)
    hit = jnp.arange(per, dtype=jnp.int32)[:, None] == slot[:, :, None, :]
    lists = jnp.sum(jnp.where(hit, code[:, :, None, :], 0), axis=3)
    return jnp.sum(number, axis=2), lists


def pair_plan(voltages, tile_of, cell_of):
    n_gx = lax.axis_size("gx")
    _, st_dev, pols, spectra, _, fine = voltages.shape
    inputs = st_dev * pols
    out_dev = fine // (n_gx * AVG)
    cells = (TILE // n_gx // BR) * (TILE // BC)
    me = lax.axis_index("grp")
    counts, lists = work_lists(tile_of, cell_of, me, out_dev, cells)
    swap = jnp.where(me == 0, jnp.arange(2), jnp.arange(2)[::-1])
    counts, lists = jnp.take(counts, swap, axis=0), jnp.take(lists, swap, axis=0)

    volts = voltages.reshape(inputs, 2, FRADIX, FRADIX).transpose(0, 2, 1, 3)
    volts = volts.reshape(inputs, 2 * FRADIX, FRADIX)
    factor = 1.0 / math.sqrt(spectra * AVG)
    tables = spectra_tables(n_gx, out_dev)
    front, middle, last = 0, out_dev // 2, out_dev - 1

    def exchange(spec):
        return lax.all_to_all(spec, "gx", split_axis=0, concat_axis=0, tiled=True)

    def swap_groups(data):
        return lax.ppermute(data, "grp", [(0, 1), (1, 0)])

    def work(grid, *items):
        number = jnp.concatenate([counts[g, start:stop] for g, start, stop, _ in items])
        list_of = jnp.concatenate([lists[g, start:stop] for g, start, stop, _ in items])
        streams = [data for _, _, _, data in items]
        return gram_call(number, list_of, streams, grid, cells, factor)

    spec_a = spectra_call(volts, tables, n_gx, out_dev, front, middle)
    mine_a = exchange(spec_a)
    spec_c = spectra_call(volts, tables, n_gx, out_dev, last, out_dev)
    other_c = swap_groups(spec_c)
    spec_b = spectra_call(volts, tables, n_gx, out_dev, middle, last)
    other_a = swap_groups(mine_a)
    mine_b = exchange(spec_b)
    grid = work(None, (0, front, middle, mine_a))
    other_b = swap_groups(mine_b)
    both_c = exchange(jnp.concatenate([spec_c, other_c], axis=1))
    grid = work(grid, (0, middle, last, mine_b), (1, front, middle, other_a))
    grid = work(grid, (1, middle, last, other_b))
    twist, second = row_tables()
    rows = rows_call(counts[:, last], lists[:, last], both_c, grid, cells, factor, twist, second, n_gx)
    data = exchange(rows)
    cos, sin = column_twist()
    image = column_call(data, column_tables(n_gx), cos, sin)
    return image.reshape(1, 2, TILE // n_gx, TILE)


def base_table(radix, sign):
    index = jnp.arange(radix, dtype=jnp.int32)
    product = index[:, None] * index[None, :] % radix
    angle = sign * 2.0 * math.pi / radix * product.astype(jnp.float32)
    return (jnp.cos(angle), jnp.sin(angle))


def twist_table(radix, sign):
    index = jnp.arange(radix, dtype=jnp.int32)
    product = index[:, None] * index[None, :]
    angle = sign * 2.0 * math.pi / (radix * radix) * product.astype(jnp.float32)
    return (jnp.cos(angle), jnp.sin(angle))


def complex_einsum(form, table, real_part, imag_part):
    cos_part, sin_part = table

    def product(left, right):
        return jnp.einsum(form, left, right, precision=lax.Precision.HIGH)

    new_real = product(cos_part, real_part) - product(sin_part, imag_part)
    new_imag = product(cos_part, imag_part) + product(sin_part, real_part)
    return (new_real, new_imag)


def fourier(real_part, imag_part, radix, sign, to_front):
    count = real_part.shape[0]
    real_part = real_part.reshape(count, radix, radix)
    imag_part = imag_part.reshape(count, radix, radix)
    table = base_table(radix, sign)
    real_part, imag_part = complex_einsum("ak,rab->rkb", table, real_part, imag_part)
    twist_cos, twist_sin = twist_table(radix, sign)
    twist_cos = twist_cos.T
    twist_sin = twist_sin.T
    turned_real = real_part * twist_cos - imag_part * twist_sin
    turned_imag = real_part * twist_sin + imag_part * twist_cos
    if to_front:
        form = "bj,rkb->jkr"
        shape = (radix * radix, count)
    else:
        form = "bj,rkb->rjk"
        shape = (count, radix * radix)
    out_real, out_imag = complex_einsum(form, table, turned_real, turned_imag)
    return (out_real.reshape(shape) / radix, out_imag.reshape(shape) / radix)


def operands(local):
    stations, pols, spectra, _, channels = local.shape
    inputs = stations * pols
    nout = channels // AVG
    grouped = local.reshape(inputs, spectra, 2, nout, AVG).transpose(3, 0, 1, 2, 4)
    swapped = jnp.stack([grouped[:, :, :, 1], -grouped[:, :, :, 0]], axis=3)
    left = jnp.stack([grouped, swapped], axis=1).reshape(nout, 2 * inputs, spectra, 2 * AVG)
    right = grouped.reshape(nout, inputs, spectra, 2 * AVG)
    return (left, right)


def gram_all(local):
    left, right = operands(local)
    nout, rows_two, spectra, depth = left.shape
    left = left.reshape(nout, rows_two, spectra * depth)
    right = right.reshape(nout, rows_two // 2, spectra * depth)
    return jnp.einsum("oyk,ork->oyr", left, right, preferred_element_type=jnp.float32)


def pair_fits(gx_count, shape):
    lead, st_dev, pols, spectra, _, fine = shape
    return (
        lead == 1
        and spectra == 1
        and fine == FRADIX * FRADIX
        and (st_dev * pols) % PACK == 0
        and fine % (gx_count * AVG) == 0
        and TILE // gx_count // BR == PACK
        and fine // (gx_count * AVG) >= 4
        and gx_count % 4 == 0
    )


def on_device(voltages, tile_of, cell_of):
    grp_count = lax.axis_size("grp")
    gx_count = lax.axis_size("gx")
    _, st_dev, pols, spectra, _, fine = voltages.shape
    if grp_count == 2 and pair_fits(gx_count, voltages.shape):
        return pair_plan(voltages, tile_of, cell_of)
    volts = voltages.reshape(st_dev * pols * spectra, 2, fine).astype(jnp.float32)
    spec_re, spec_im = fourier(volts[:, 0], volts[:, 1], FRADIX, -1.0, False)
    spec = jnp.stack([spec_re, spec_im], axis=1).astype(jnp.bfloat16)
    spec = spec.reshape(st_dev, pols, spectra, 2, fine)
    local = lax.all_to_all(spec, "gx", split_axis=4, concat_axis=0, tiled=True)
    gram = gram_all(local)
    factor = 1.0 / math.sqrt(spectra * AVG)
    out_dev = gram.shape[0]
    inputs = gram.shape[2]
    vis = (gram * factor).astype(jnp.bfloat16).reshape(out_dev, 2, inputs, inputs)
    width = 2 * BR * BC
    shaped = vis.reshape(out_dev, 2, inputs // BR, BR, inputs // BC, BC)
    blocks = shaped.transpose(0, 2, 4, 1, 3, 5).reshape(-1, width)
    count_blocks = blocks.shape[0]
    capacity = max(2, count_blocks // (4 * grp_count))
    slots = grp_count * capacity
    me = lax.axis_index("grp")
    groups = tile_of.shape[0]
    marked = (tile_of[:, None, :] == jnp.arange(grp_count, dtype=jnp.int32)[None, :, None]).astype(
        jnp.int32
    )
    rank_all = jnp.sum((jnp.cumsum(marked, axis=2) - marked) * marked, axis=1)
    my_tiles = lax.dynamic_index_in_dim(tile_of, me, 0, keepdims=False)
    my_rank = lax.dynamic_index_in_dim(rank_all, me, 0, keepdims=False)
    slot_id = jnp.where(my_tiles < 0, -1, my_tiles * capacity + my_rank)
    hits = jnp.arange(slots, dtype=jnp.int32)[:, None] == slot_id[None, :]
    filled = jnp.any(hits, axis=1)
    source = jnp.where(filled, jnp.argmax(hits, axis=1), count_blocks)
    padded = jnp.concatenate([blocks, jnp.zeros((1, width), jnp.bfloat16)], axis=0)
    outgoing = jnp.take(padded, source, axis=0)
    outgoing = outgoing.reshape(grp_count, capacity, width)
    arrived = lax.all_to_all(outgoing, "grp", split_axis=0, concat_axis=0, tiled=True)
    slab = TILE // gx_count
    row_blocks = slab // BR
    col_blocks = TILE // BC
    cells_count = row_blocks * col_blocks
    source_group = jnp.arange(groups, dtype=jnp.int32)[:, None]
    slot_flat = jnp.where(tile_of == me, source_group * capacity + rank_all, -1).reshape(-1)
    cell_flat = cell_of.reshape(-1)
    cell_hit = (jnp.arange(cells_count, dtype=jnp.int32)[:, None] == cell_flat[None, :]).astype(
        jnp.bfloat16
    )
    slot_hit = (jnp.arange(slots, dtype=jnp.int32)[:, None] == slot_flat[None, :]).astype(
        jnp.bfloat16
    )
    place = lax.dot_general(
        cell_hit, slot_hit, (((1,), (1,)), ((), ())), preferred_element_type=jnp.float32
    )
    place = place.astype(jnp.bfloat16)
    grid = jnp.dot(place, arrived.reshape(slots, width), preferred_element_type=jnp.float32)
    grid = (
        grid.reshape(row_blocks, col_blocks, 2, BR, BC)
        .transpose(2, 0, 3, 1, 4)
        .reshape(2, slab, TILE)
    )
    rows_re, rows_im = fourier(grid[0], grid[1], TRADIX, 1.0, True)
    rows = jnp.stack([rows_re, rows_im], axis=0).astype(jnp.bfloat16)
    columns = lax.all_to_all(rows, "gx", split_axis=1, concat_axis=2, tiled=True)
    kx_local = columns.shape[1]
    image_re, image_im = fourier(
        columns[0].astype(jnp.float32), columns[1].astype(jnp.float32), TRADIX, 1.0, False
    )
    image = jnp.stack([image_re, image_im], axis=0).reshape(1, 2, kx_local, TILE)
    return image


def solution(mesh):
    in_specs = (P("grp", "gx", None, None, None, None), P(None, "gx"), P(None, "gx"))
    out_specs = P("grp", None, "gx", None)
    return jax.shard_map(
        on_device, mesh=mesh, in_specs=in_specs, out_specs=out_specs, check_vma=False
    )
```
